32 devices in a mesh: seq: 8 (over z, x), head: 4 (over y, core).
Axes of the slice: x: 2, y: 2, z: 4, core: 2. Of those that a mesh axis runs over, the one named last changes fastest.
Arguments:
- block_input: bfloat16 [4096, 2048], P(('seq', 'head')), may hold values from -6 to 6
- norm1_gain: float32 [2048], replicated, may hold values from 0.5 to 1.5
- query_weight: bfloat16 [2048, 2048], P(None, 'head'), may hold values from -0.125 to 0.125
- key_weight: bfloat16 [2048, 2048], P(None, 'head'), may hold values from -0.125 to 0.125
- value_weight: bfloat16 [2048, 2048], P(None, 'head'), may hold values from -0.125 to 0.125
- gate_weight: bfloat16 [2048, 2048], P(None, 'head'), may hold values from -0.125 to 0.125
- rate_weight: bfloat16 [2048, 32], P(None, 'head'), may hold values from -0.125 to 0.125
- rate_bias: float32 [32], P('head'), may hold values from -3 to 3
- rate_scale: float32 [32], P('head'), may hold values from 7.324219e-05 to 0.008
- init_state: float32 [32, 64, 64], P('head'), may hold values from -0.75 to 0.75
- init_bias: float32 [32, 64], P('head'), may hold values from -5 to 5
- post_gain: float32 [2048], P('head'), may hold values from 0.5 to 1.5
- post_bias: float32 [2048], P('head'), may hold values from -3 to 3
- out_weight: bfloat16 [2048, 2048], P('head'), may hold values from -0.25 to 0.25
- norm2_gain: float32 [2048], replicated, may hold values from 0.5 to 1.5
- mlp_gate: bfloat16 [2048, 5504], P(None, 'head'), may hold values from -0.125 to 0.125
- mlp_up: bfloat16 [2048, 5504], P(None, 'head'), may hold values from -0.125 to 0.125
- mlp_down: bfloat16 [5504, 2048], P('head'), may hold values from -0.15625 to 0.15625
- out_cotangent: bfloat16 [4096, 2048], P(('seq', 'head')), may hold values from -6 to 6
Outputs:
- block_out: bfloat16 [4096, 2048], P(('seq', 'head'))
- input_grad: float32 [4096, 2048], P(('seq', 'head'))
- norm1_gain_grad: float32 [2048], replicated
- query_weight_grad: float32 [2048, 2048], P(None, 'head')
- key_weight_grad: float32 [2048, 2048], P(None, 'head')
- value_weight_grad: float32 [2048, 2048], P(None, 'head')
- gate_weight_grad: float32 [2048, 2048], P(None, 'head')
- rate_weight_grad: float32 [2048, 32], P(None, 'head')
- rate_bias_grad: float32 [32], P('head')
- rate_scale_grad: float32 [32], P('head')
- init_state_grad: float32 [32, 64, 64], P('head')
- init_bias_grad: float32 [32, 64], P('head')
- post_gain_grad: float32 [2048], P('head')
- post_bias_grad: float32 [2048], P('head')
- out_weight_grad: float32 [2048, 2048], P('head')
- norm2_gain_grad: float32 [2048], replicated
- mlp_gate_grad: float32 [2048, 5504], P(None, 'head')
- mlp_up_grad: float32 [2048, 5504], P(None, 'head')
- mlp_down_grad: float32 [5504, 2048], P('head')
The draws below stay inside these ranges and needn't reach their ends.
All inputs are finite; a program needn't handle non-finite values.
Results may differ from the reference program's by a relative error of at most 0.025.
Values may be sent and summed in bfloat16 or wider, within the bound.
No kernel may reach another device: no remote copies, remote signals or barrier semaphores. Data moves between devices by JAX's collectives and lax.ppermute only.
A program may use at most 256 MiB of HBM per device.

```python
import math
import jax
import jax.numpy as jnp
from jax import lax

D = 2048
H = 32
HD = 64
FF = 5504
MB = 16
TOKENS = 4096


def block_levels(rng, shape, shards, least, largest):
    factor_of = 1.0
    for axis_at, blocks in shards:
        heights = jax.random.uniform(jax.random.fold_in(jax.random.fold_in(rng, 6), axis_at), (blocks,), jnp.float32, least / len(shards), largest / len(shards))
        factor_of = factor_of * jnp.repeat(jnp.exp(heights), shape[axis_at] // blocks).reshape((-1,) + (1,) * (len(shape) - 1 - axis_at))
    return factor_of


def noise(own_key, extent, deviation, most, pieces=(), dtype=jnp.bfloat16):
    level = block_levels(own_key, extent, pieces, -0.22, 0.18) if pieces else 1.0
    result = jax.random.normal(own_key, extent, jnp.float32) * deviation * level
    return jnp.minimum(jnp.maximum(result, -most), most).astype(dtype)


def setup_inputs(seed: int = 0) -> dict:
    streams_of = jax.random.split(jax.random.key(seed), 20)
    block_input = noise(streams_of[0], (TOKENS, D), 1.0, 6.0, ((0, 32),))
    norm1_gain = jnp.clip(1.0 + 0.1 * jax.random.normal(streams_of[1], (D,), jnp.float32), 0.5, 1.5)
    query_weight = noise(streams_of[2], (D, D), D ** -0.5, 0.125, ((1, 4),))
    key_weight = noise(streams_of[3], (D, D), D ** -0.5, 0.125, ((1, 4),))
    value_weight = noise(streams_of[4], (D, D), D ** -0.5, 0.125, ((1, 4),))
    gate_weight = noise(streams_of[5], (D, D), D ** -0.5, 0.125, ((1, 4),))
    rate_weight = noise(streams_of[6], (D, H), D ** -0.5, 0.125, ((1, 4),))
    rate_bias = noise(streams_of[7], (H,), 1.0, 3.0, ((0, 4),), jnp.float32)
    rate_scale = jnp.clip(jnp.exp(math.log(0.008) - 4.693425 * jax.random.uniform(streams_of[8], (H,), jnp.float32) ** block_levels(streams_of[8], (H,), ((0, 4),), -0.2, 0.2)), 7.324219041038305e-05, 0.008)
    init_state = noise(streams_of[9], (H, HD, HD), HD ** -0.5, 0.75, ((0, 4),), jnp.float32)
    init_bias = noise(streams_of[10], (H, HD), 1.0, 5.0, ((0, 4),), jnp.float32)
    post_gain = jnp.clip(1.0 + 0.1 * jax.random.normal(streams_of[11], (D,), jnp.float32), 0.5, 1.5)
    post_bias = noise(streams_of[12], (D,), 0.5, 3.0, ((0, 4),), jnp.float32)
    out_weight = noise(streams_of[13], (D, D), (D // 4) ** -0.5, 0.25, ((0, 4),))
    norm2_gain = jnp.clip(1.0 + 0.1 * jax.random.normal(streams_of[14], (D,), jnp.float32), 0.5, 1.5)
    mlp_gate = noise(streams_of[15], (D, FF), D ** -0.5, 0.125, ((1, 4),))
    mlp_up = noise(streams_of[16], (D, FF), D ** -0.5, 0.125, ((1, 4),))
    mlp_down = noise(streams_of[17], (FF, D), (FF // 4) ** -0.5, 0.15625, ((0, 4),))
    out_cotangent = noise(streams_of[18], (TOKENS, D), 1.0, 6.0, ((0, 32),))
    return dict(block_input=block_input, norm1_gain=norm1_gain, query_weight=query_weight, key_weight=key_weight, value_weight=value_weight, gate_weight=gate_weight, rate_weight=rate_weight, rate_bias=rate_bias, rate_scale=rate_scale, init_state=init_state, init_bias=init_bias, post_gain=post_gain, post_bias=post_bias, out_weight=out_weight, norm2_gain=norm2_gain, mlp_gate=mlp_gate, mlp_up=mlp_up, mlp_down=mlp_down, out_cotangent=out_cotangent)


@jax.custom_vjp
def low(v):
    return lax.optimization_barrier(v.astype(jnp.bfloat16)).astype(jnp.float32)

@jax.custom_vjp
def low_back(v):
    return v

def low_keep(v):
    return (low(v), None)

def low_pass(kept, grad):
    return (grad,)

def back_keep(v):
    return (v, None)

def back_low(kept, grad):
    return (low(grad),)
low.defvjp(low_keep, low_pass)
low_back.defvjp(back_keep, back_low)
HIGHEST = lax.Precision.HIGHEST
EPSILON = 1e-06

def matmul(left, right):
    return jnp.dot(left, right, precision=HIGHEST)

def rms_unit(values):
    return values * lax.rsqrt(lax.optimization_barrier(jnp.mean(values * values, axis=-1, keepdims=True)) + EPSILON)

def gelu_tanh(values):
    return jax.nn.gelu(values, approximate=True)

def augment(values):
    ones_col = jnp.ones(values.shape[:-1] + (1,), jnp.float32)
    return jnp.concatenate([values, ones_col], axis=-1)

def inner_block(inner_state, inputs):
    query_rows, key_rows, value_rows, rate_rows = inputs
    query_aug = augment(query_rows)
    key_aug = augment(key_rows)
    errors = jnp.einsum('hmi,hio->hmo', key_aug, inner_state, precision=HIGHEST) - (value_rows - key_rows)
    scores = jnp.einsum('hmi,hni->hmn', query_aug, key_aug, precision=HIGHEST)
    causal_mask = jnp.tril(jnp.ones((scores.shape[1], scores.shape[2]), jnp.float32))
    weighted = scores * causal_mask * rate_rows[:, None, :]
    outputs = query_rows + jnp.einsum('hmi,hio->hmo', query_aug, inner_state, precision=HIGHEST) - jnp.einsum('hmn,hno->hmo', weighted, errors, precision=HIGHEST)
    new_state = inner_state - jnp.einsum('hni,hno->hio', key_aug * rate_rows[:, :, None], errors, precision=HIGHEST)
    return (new_state, outputs)

def to_heads(values):
    return values.reshape(TOKENS // MB, MB, H, HD).transpose(0, 2, 1, 3)

def forward(block_input, norm1_gain, query_weight, key_weight, value_weight, gate_weight, rate_weight, rate_bias, rate_scale, init_state, init_bias, post_gain, post_bias, out_weight, norm2_gain, mlp_gate, mlp_up, mlp_down):
    normed = low(rms_unit(block_input) * norm1_gain)
    query_rows = low_back(matmul(normed, query_weight))
    key_rows = low_back(matmul(normed, key_weight))
    value_rows = low_back(matmul(normed, value_weight))
    gate_pre = low_back(matmul(normed, gate_weight))
    rate_pre = low_back(matmul(normed, rate_weight) + rate_bias)
    rate_rows = jax.nn.sigmoid(rate_pre) * rate_scale
    rate_blocks = rate_rows.reshape(TOKENS // MB, MB, H).transpose(0, 2, 1)
    start_state = jnp.concatenate([init_state, init_bias[:, None, :]], axis=1)
    last_state, z_blocks = lax.scan(jax.checkpoint(inner_block), start_state, (to_heads(query_rows), to_heads(key_rows), to_heads(value_rows), rate_blocks))
    z_rows = z_blocks.transpose(0, 2, 1, 3).reshape(TOKENS, D)
    row_mean = lax.optimization_barrier(jnp.mean(z_rows, axis=-1, keepdims=True))
    centered = z_rows - row_mean
    row_var = lax.optimization_barrier(jnp.mean(centered * centered, axis=-1, keepdims=True))
    post_out = centered * lax.rsqrt(row_var + EPSILON) * post_gain + post_bias
    gated_out = low(gelu_tanh(gate_pre) * post_out)
    middle = block_input + low_back(matmul(gated_out, out_weight))
    mlp_input = low(rms_unit(middle) * norm2_gain)
    gate_mlp = low_back(matmul(mlp_input, mlp_gate))
    up_mlp = low_back(matmul(mlp_input, mlp_up))
    hidden = low(jax.nn.silu(gate_mlp) * up_mlp)
    return middle + low_back(matmul(hidden, mlp_down))

def reference(block_input, norm1_gain, query_weight, key_weight, value_weight, gate_weight, rate_weight, rate_bias, rate_scale, init_state, init_bias, post_gain, post_bias, out_weight, norm2_gain, mlp_gate, mlp_up, mlp_down, out_cotangent):
    arguments = tuple((array_in.astype(jnp.float32) for array_in in (block_input, norm1_gain, query_weight, key_weight, value_weight, gate_weight, rate_weight, rate_bias, rate_scale, init_state, init_bias, post_gain, post_bias, out_weight, norm2_gain, mlp_gate, mlp_up, mlp_down)))
    block_out, pullback = jax.vjp(forward, *arguments)
    gradients = pullback(out_cotangent.astype(jnp.float32))
    return (block_out.astype(jnp.bfloat16), gradients[0], gradients[1], gradients[2], gradients[3], gradients[4], gradients[5], gradients[6], gradients[7], gradients[8], gradients[9], gradients[10], gradients[11], gradients[12], gradients[13], gradients[14], gradients[15], gradients[16], gradients[17])
```

```python
import functools
import jax, jax.numpy as jnp
from jax import lax
from jax.experimental import pallas as pl
from jax.experimental.pallas import tpu as pltpu
from jax.sharding import PartitionSpec as P

CHUNK=128
MB=16
F32=jnp.float32; BF=jnp.bfloat16
LN=128
HW=64
VL=48*1024*1024

def mm(a,b,ca,cb):
    return lax.dot_general(a.astype(BF),b.astype(BF),(((ca,),(cb,)),((),())),preferred_element_type=F32)
def nn(a,b): return mm(a,b,1,0)
def nt(a,b): return mm(a,b,1,1)
def tn(a,b): return mm(a,b,0,0)
def split(a):
    hi=a.astype(BF)
    return hi,(a-hi.astype(F32)).astype(BF)
def nn3(a,b):
    ah,al=a; bh,bl=b
    return nn(ah,bh)+(nn(ah,bl)+nn(al,bh))

def lanes(shape): return lax.broadcasted_iota(jnp.int32,shape,1)
def rows(shape): return lax.broadcasted_iota(jnp.int32,shape,0)
def head_of(x,odd):
    y=pltpu.roll(x,HW,1) if odd else x
    return jnp.where(lanes(x.shape)<HW,y,0.0)
def aug(x): return jnp.where(lanes(x.shape)==HW,1.0,x)
def pair(a,b):
    return jnp.where(lanes(a.shape)<HW,a,pltpu.roll(b,HW,1))
def column(block,h):
    return jnp.sum(jnp.where(lanes(block.shape)==h,block,0.0),axis=1,keepdims=True)
def causal(C): return rows((C,C))>=lanes((C,C))
def earlier(C): return (rows((C,C))//MB)>(lanes((C,C))//MB)
def level(C,size):
    i=rows((C,C)); j=lanes((C,C))
    return (i//(2*size)==j//(2*size))&((i//size)%2==1)&((j//size)%2==0)

def block_inverse(low,C):
    eye=jnp.where(rows((C,C))==lanes((C,C)),1.0,0.0)
    size=MB
    t=eye-jnp.where(level(C,size),low,0.0)
    size*=2
    while size<C:
        part=split(jnp.where(level(C,size),low,0.0))
        ts=split(t)
        t=t-nn3(split(nn3(ts,part)),ts)
        size*=2
    return t

def map_kernel(C,k_ref,v_ref,r_ref,t_ref,uw_ref,x_ref,y_ref):
    p=pl.program_id(0)
    N=k_ref.shape[0]
    last=y_ref.shape[0]-1
    @pl.when(p==0)
    def _(): y_ref[last]=jnp.zeros((80,LN),BF)
    for odd in range(2):
        h=2*p+odd
        total=None
        for c in range(N//C):
            sl=pl.ds(c*C,C)
            k=head_of(k_ref[sl,:],odd)
            w=head_of(v_ref[sl,:],odd)-k
            ka=aug(k)
            r=column(r_ref[sl,:],h)
            kr=ka*r
            t=block_inverse(jnp.where(earlier(C),nt(ka,kr),0.0),C)
            t_ref[odd,c]=t.astype(BF)
            uw=nn(t,jnp.concatenate([ka,w],axis=1))
            uw_ref[odd,sl,:]=uw.astype(BF)
            xc=tn(kr,jnp.where(lanes(uw.shape)<LN,-uw,uw))
            x_ref[odd,c]=xc.astype(BF)
            total=xc if total is None else total+xc+nn(xc[:,:LN],total)
        a=total[:,:LN]; o=total[:,LN:]
        y_ref[h]=pair(a,o)[:80].astype(BF)
        col=jnp.sum(jnp.where(lanes(a.shape)==HW,a,0.0),axis=1,keepdims=True)[:80]
        y_ref[last]=jnp.where(lanes((80,LN))==h,col,y_ref[last].astype(F32)).astype(BF)

def local_kernel(C,q_ref,k_ref,r_ref,t_ref,uw_ref,qe_ref,zo_ref,pt_ref,vv_ref):
    p=pl.program_id(0)
    N=q_ref.shape[0]
    for c in range(N//C):
        sl=pl.ds(c*C,C)
        offs=[]
        for odd in range(2):
            h=2*p+odd
            q=head_of(q_ref[sl,:],odd); qa=aug(q)
            ka=aug(head_of(k_ref[sl,:],odd))
            kr=ka*column(r_ref[sl,:],h)
            pm=jnp.where(causal(C),nt(qa,kr),0.0)
            t=t_ref[odd,c]
            puw=nn(pm,uw_ref[odd,sl,:])
            qe_ref[odd,sl,:]=(qa-puw[:,:LN]).astype(BF)
            offs.append(q+puw[:,LN:])
            pt_ref[odd,c]=nn(pm,t).astype(BF)
            vv_ref[odd,sl,:]=tn(t,kr).astype(BF)
        zo_ref[sl,:]=pair(offs[0],offs[1])

def unpack(y,yb,h):
    y=y.astype(F32)
    col=column(yb.astype(F32),h)
    ln=lanes(y.shape)
    a=jnp.where(ln<HW,y,jnp.where(ln==HW,col,0.0))
    o=jnp.where(ln<HW,pltpu.roll(y,HW,1),0.0)
    pad=jnp.zeros((LN-80,LN),F32)
    return jnp.concatenate([a,pad],0),jnp.concatenate([o,pad],0)

def start_of(is_ref,ib_ref,odd):
    s=jnp.concatenate([is_ref[odd],ib_ref[odd],jnp.zeros((LN-HW-1,HW),F32)],axis=0)
    return jnp.concatenate([s,jnp.zeros_like(s)],axis=1)

def forward_kernel(C,seg_ref,y_ref,yb_ref,is_ref,ib_ref,x_ref,uw_ref,qe_ref,zo_ref,z_ref,e_ref,s_ref):
    p=pl.program_id(0)
    N=zo_ref.shape[0]
    segs=y_ref.shape[0]
    seg=seg_ref[0]
    add=[[None]*(N//C) for _ in range(2)]
    for odd in range(2):
        h=2*p+odd
        s=start_of(is_ref,ib_ref,odd)
        for j in range(segs-1):
            a,o=unpack(y_ref[j,odd],yb_ref[j,0],h)
            s=s+jnp.where(j<seg,1.0,0.0)*(nn(a,s)+o)
        for c in range(N//C):
            sl=pl.ds(c*C,C)
            sb=s.astype(BF)
            s_ref[odd,c]=sb
            uw=uw_ref[odd,sl,:]
            e_ref[odd,sl,:]=(nn(uw[:,:LN],sb)-uw[:,LN:].astype(F32)).astype(BF)
            add[odd][c]=nn(qe_ref[odd,sl,:],sb)
            x=x_ref[odd,c]
            s=s+nn(x[:,:LN],sb)+x[:,LN:].astype(F32)
    for c in range(N//C):
        sl=pl.ds(c*C,C)
        z_ref[sl,:]=zo_ref[sl,:]+pair(add[0][c],add[1][c])

def state_grad_kernel(C,dz_ref,qe_ref,x_ref,d_ref,dseg_ref):
    N=dz_ref.shape[0]
    outs=[]
    for odd in range(2):
        g=jnp.zeros((LN,LN),F32)
        for c in reversed(range(N//C)):
            sl=pl.ds(c*C,C)
            dz=head_of(dz_ref[sl,:],odd)
            d=tn(qe_ref[odd,sl,:],dz)
            d_ref[odd,c]=d
            g=g+tn(x_ref[odd,c][:,:LN],g)+d
        outs.append(g)
    dseg_ref[0]=pair(outs[0],outs[1])[:72]

def query_grad_kernel(C,q_ref,k_ref,r_ref,dz_ref,e_ref,s_ref,pt_ref,dq_ref,b_ref,l_ref):
    p=pl.program_id(0)
    N=q_ref.shape[0]
    for c in range(N//C):
        sl=pl.ds(c*C,C)
        outs=[]
        for odd in range(2):
            h=2*p+odd
            dz=head_of(dz_ref[sl,:],odd); dzb=dz.astype(BF)
            qa=aug(head_of(q_ref[sl,:],odd))
            ka=aug(head_of(k_ref[sl,:],odd))
            kr=ka*column(r_ref[sl,:],h)
            fu=jnp.where(causal(C),-nt(dzb,e_ref[odd,sl,:]),0.0).astype(BF)
            outs.append(dz+nt(dzb,s_ref[odd,c])+nn(fu,kr))
            b_ref[odd,sl,:]=tn(fu,qa).astype(BF)
            l_ref[odd,sl,:]=-tn(pt_ref[odd,c],dzb)
        dq_ref[sl,:]=pair(outs[0],outs[1]).astype(BF)

def key_grad_kernel(C,seg_ref,y_ref,yb_ref,da_ref,k_ref,r_ref,e_ref,s_ref,vv_ref,b_ref,l_ref,x_ref,d_ref,dk_ref,dv_ref,dr_ref,gi_ref):
    p=pl.program_id(0)
    N=k_ref.shape[0]
    segs=y_ref.shape[0]
    seg=seg_ref[0]
    @pl.when(p==0)
    def _(): dr_ref[...]=jnp.zeros_like(dr_ref)
    pad=jnp.zeros((LN-72,LN),F32)
    dks=[[None]*(N//C) for _ in range(2)]
    lams=[[None]*(N//C) for _ in range(2)]
    for odd in range(2):
        h=2*p+odd
        full=jnp.zeros((LN,LN),F32)
        g=jnp.zeros((LN,LN),F32)
        for j in reversed(range(segs)):
            a,_=unpack(y_ref[j,odd],yb_ref[j,0],h)
            d=jnp.concatenate([head_of(da_ref[j,0],odd),pad],0)
            full=full+tn(a,full)+d
            g=jnp.where(j==seg+1,full,g)
        gi_ref[odd]=full[:72]
        for c in reversed(range(N//C)):
            sl=pl.ds(c*C,C)
            gb=g.astype(BF)
            ka=aug(head_of(k_ref[sl,:],odd))
            r=column(r_ref[sl,:],h)
            kr=ka*r
            e=e_ref[odd,sl,:]
            lam=l_ref[odd,sl,:]-nn(vv_ref[odd,sl,:],gb)
            lb=lam.astype(BF)
            hu=jnp.where(earlier(C),-nt(lb,e),0.0).astype(BF)
            b=b_ref[odd,sl,:].astype(F32)+tn(hu,ka)-nt(e,gb)
            dks[odd][c]=r*b+nt(lb,s_ref[odd,c])+nn(hu,kr)+lam
            lams[odd][c]=lam
            dr=jnp.sum(ka*b,axis=1,keepdims=True)
            dr_ref[sl,:]=jnp.where(lanes((C,dr_ref.shape[1]))==h,dr,dr_ref[sl,:])
            g=g+tn(x_ref[odd,c][:,:LN],gb)+d_ref[odd,c]
    for c in range(N//C):
        sl=pl.ds(c*C,C)
        dk_ref[sl,:]=pair(dks[0][c],dks[1][c]).astype(BF)
        dv_ref[sl,:]=-pair(lams[0][c],lams[1][c]).astype(BF)

def params(): return pltpu.CompilerParams(dimension_semantics=("arbitrary",),vmem_limit_bytes=VL)
def S(shape,dt): return jax.ShapeDtypeStruct(shape,dt)

def specs(N,hl,C):
    nc=N//C
    d={}
    d["row"]=pl.BlockSpec((N,LN),lambda p,*_:(0,p))
    d["rate"]=pl.BlockSpec((N,hl),lambda p,*_:(0,0))
    d["cc"]=pl.BlockSpec((2,nc,C,C),lambda p,*_:(p,0,0,0))
    d["n256"]=pl.BlockSpec((2,N,2*LN),lambda p,*_:(p,0,0))
    d["n128"]=pl.BlockSpec((2,N,LN),lambda p,*_:(p,0,0))
    d["x"]=pl.BlockSpec((2,nc,LN,2*LN),lambda p,*_:(p,0,0,0))
    d["s"]=pl.BlockSpec((2,nc,LN,LN),lambda p,*_:(p,0,0,0))
    d["y"]=pl.BlockSpec((hl+1,80,LN),lambda p,*_:(0,0,0))
    return d

def build(N,hl,segs,C=128):
    nc=N//C; sp=specs(N,hl,C); G=(hl//2,)
    w=hl*HW
    K={}
    K["map"]=pl.pallas_call(functools.partial(map_kernel,C),grid=G,in_specs=[sp["row"],sp["row"],sp["rate"]],
        out_specs=[sp["cc"],sp["n256"],sp["x"],sp["y"]],
        out_shape=[S((hl,nc,C,C),BF),S((hl,N,2*LN),BF),S((hl,nc,LN,2*LN),BF),S((hl+1,80,LN),BF)],compiler_params=params(),name="segment_maps")
    K["local"]=pl.pallas_call(functools.partial(local_kernel,C),grid=G,in_specs=[sp["row"],sp["row"],sp["rate"],sp["cc"],sp["n256"]],
        out_specs=[sp["n128"],sp["row"],sp["cc"],sp["n128"]],
        out_shape=[S((hl,N,LN),BF),S((N,w),F32),S((hl,nc,C,C),BF),S((hl,N,LN),BF)],compiler_params=params(),name="local_parts")
    yall=pl.BlockSpec((segs,2,80,LN),lambda p,*_:(0,p,0,0)); yball=pl.BlockSpec((segs,1,80,LN),lambda p,*_:(0,hl,0,0))
    dall=pl.BlockSpec((segs,1,72,LN),lambda p,*_:(0,p,0,0))
    ist=pl.BlockSpec((2,HW,HW),lambda p,*_:(p,0,0)); ibs=pl.BlockSpec((2,1,HW),lambda p,*_:(p,0,0))
    def gs(i,o): return pltpu.PrefetchScalarGridSpec(num_scalar_prefetch=1,grid=G,in_specs=i,out_specs=o)
    K["forward"]=pl.pallas_call(functools.partial(forward_kernel,C),grid_spec=gs([yall,yball,ist,ibs,sp["x"],sp["n256"],sp["n128"],sp["row"]],[sp["row"],sp["n128"],sp["s"]]),
        out_shape=[S((N,w),F32),S((hl,N,LN),BF),S((hl,nc,LN,LN),BF)],compiler_params=params(),name="forward_states")
    K["sgrad"]=pl.pallas_call(functools.partial(state_grad_kernel,C),grid=G,in_specs=[sp["row"],sp["n128"],sp["x"]],
        out_specs=[sp["s"],pl.BlockSpec((1,72,LN),lambda p:(p,0,0))],out_shape=[S((hl,nc,LN,LN),F32),S((hl//2,72,LN),F32)],compiler_params=params(),name="state_grads")
    K["qgrad"]=pl.pallas_call(functools.partial(query_grad_kernel,C),grid=G,in_specs=[sp["row"],sp["row"],sp["rate"],sp["row"],sp["n128"],sp["s"],sp["cc"]],
        out_specs=[sp["row"],sp["n128"],sp["n128"]],out_shape=[S((N,w),BF),S((hl,N,LN),BF),S((hl,N,LN),F32)],compiler_params=params(),name="query_grads")
    K["kgrad"]=pl.pallas_call(functools.partial(key_grad_kernel,C),grid_spec=gs([yall,yball,dall,sp["row"],sp["rate"],sp["n128"],sp["s"],sp["n128"],sp["n128"],sp["n128"],sp["x"],sp["s"]],
        [sp["row"],sp["row"],sp["rate"],pl.BlockSpec((2,72,LN),lambda p,*_:(p,0,0))]),
        out_shape=[S((N,w),BF),S((N,w),BF),S((N,hl),F32),S((hl,72,LN),F32)],compiler_params=params(),name="key_grads")
    return K


EPSILON = 1e-06


def gelu_tanh(values):
    return jax.nn.gelu(values, approximate=True)


def dot(a, b):
    return jnp.dot(a, b, preferred_element_type=F32)


def body(
    block_input,
    norm1_gain,
    query_weight,
    key_weight,
    value_weight,
    gate_weight,
    rate_weight,
    rate_bias,
    rate_scale,
    init_state,
    init_bias,
    post_gain,
    post_bias,
    out_weight,
    norm2_gain,
    mlp_gate,
    mlp_up,
    mlp_down,
    out_cotangent,
):
    local_heads = init_state.shape[0]
    head_width = init_state.shape[1]
    model_width = block_input.shape[1]
    seq_index = lax.axis_index("seq")
    segs = lax.axis_size("seq")
    tokens = block_input.shape[0] * lax.axis_size("head")
    K = build(tokens, local_heads, segs, CHUNK)
    seg = seq_index.astype(jnp.int32).reshape(1)

    input_f32 = block_input.astype(F32)
    scale_in = lax.rsqrt(jnp.mean(input_f32 * input_f32, axis=-1, keepdims=True) + EPSILON)
    unit_in = input_f32 * scale_in
    normed = (unit_in * norm1_gain).astype(BF)
    group_in = lax.all_gather(normed, "head", axis=0, tiled=True)
    group_cot = lax.all_gather(out_cotangent, "head", axis=0, tiled=True)
    query_rows = dot(group_in, query_weight)
    key_rows = dot(group_in, key_weight)
    value_rows = dot(group_in, value_weight)
    gate_pre = dot(group_in, gate_weight)
    rate_pre = dot(group_in, rate_weight) + rate_bias
    rate_sig = jax.nn.sigmoid(rate_pre)
    rate_rows = rate_sig * rate_scale

    inv, uw, step_maps, seg_map = K["map"](key_rows, value_rows, rate_rows)
    all_maps = lax.all_gather(seg_map, "seq", axis=0, tiled=False)
    q_eff, z_off, pt, vv = K["local"](query_rows, key_rows, rate_rows, inv, uw)
    z_rows, errors, states = K["forward"](
        seg, all_maps, all_maps, init_state, init_bias[:, None, :], step_maps, uw, q_eff, z_off
    )
    stat_sums = lax.psum((jnp.sum(z_rows, axis=-1), jnp.sum(z_rows * z_rows, axis=-1)), "head")
    row_mean = stat_sums[0] / model_width
    row_var = stat_sums[1] / model_width - row_mean * row_mean
    inv_scale = lax.rsqrt(row_var + EPSILON)[:, None]
    z_hat = (z_rows - row_mean[:, None]) * inv_scale
    post_out = z_hat * post_gain + post_bias
    gate_act, gelu_back = jax.vjp(gelu_tanh, gate_pre)
    gated_out = (gate_act * post_out).astype(BF)
    attn_out = lax.psum_scatter(
        dot(gated_out, out_weight).astype(BF), "head", scatter_dimension=0, tiled=True
    ).astype(F32)
    middle = input_f32 + attn_out
    scale_mid = lax.rsqrt(jnp.mean(middle * middle, axis=-1, keepdims=True) + EPSILON)
    unit_mid = middle * scale_mid
    mlp_input = (unit_mid * norm2_gain).astype(BF)
    mlp_group = lax.all_gather(mlp_input, "head", axis=0, tiled=True)
    gate_mlp = dot(mlp_group, mlp_gate)
    up_mlp = dot(mlp_group, mlp_up)
    silu_gate, silu_back = jax.vjp(jax.nn.silu, gate_mlp)
    hidden = (silu_gate * up_mlp).astype(BF)
    mlp_out = lax.psum_scatter(
        dot(hidden, mlp_down).astype(BF), "head", scatter_dimension=0, tiled=True
    ).astype(F32)
    block_out = (middle + mlp_out).astype(BF)
    cot_f32 = out_cotangent.astype(F32)
    d_hidden = dot(group_cot, mlp_down.T)
    mlp_down_grad = dot(hidden.T, group_cot)
    d_gate_mlp = silu_back(d_hidden * up_mlp)[0].astype(BF)
    d_up_mlp = (d_hidden * silu_gate).astype(BF)
    mlp_gate_grad = dot(mlp_group.T, d_gate_mlp)
    mlp_up_grad = dot(mlp_group.T, d_up_mlp)
    mlp_sums = lax.psum(
        (mlp_down_grad.astype(BF), mlp_gate_grad.astype(BF), mlp_up_grad.astype(BF)), "seq"
    )
    d_mlp_input = lax.psum_scatter(
        (dot(d_gate_mlp, mlp_gate.T) + dot(d_up_mlp, mlp_up.T)).astype(BF),
        "head",
        scatter_dimension=0,
        tiled=True,
    ).astype(F32)
    scaled_mid = d_mlp_input * norm2_gain
    norm2_part = jnp.sum(d_mlp_input * unit_mid, axis=0)
    d_middle = cot_f32 + scale_mid * (
        scaled_mid - unit_mid * jnp.mean(scaled_mid * unit_mid, axis=-1, keepdims=True)
    )
    d_attn = d_middle.astype(BF)
    d_attn_group = lax.all_gather(d_attn, "head", axis=0, tiled=True)
    d_gated = dot(d_attn_group, out_weight.T)
    out_weight_grad = dot(gated_out.T, d_attn_group)
    d_post = d_gated * gate_act
    d_gate_pre = gelu_back(d_gated * post_out)[0].astype(BF)
    post_gain_part = jnp.sum(d_post * z_hat, axis=0)
    post_bias_part = jnp.sum(d_post, axis=0)
    d_zhat = d_post * post_gain
    back_sums = lax.psum((jnp.sum(d_zhat, axis=-1), jnp.sum(d_zhat * z_hat, axis=-1)), "head")
    d_z = inv_scale * (
        d_zhat - back_sums[0][:, None] / model_width - z_hat * (back_sums[1][:, None] / model_width)
    )
    step_grads, seg_grad = K["sgrad"](d_z, q_eff, step_maps)
    all_grads = lax.all_gather(seg_grad, "seq", axis=0, tiled=False)
    d_query, b_part, lam_part = K["qgrad"](query_rows, key_rows, rate_rows, d_z, errors, states, pt)
    d_key, d_value, d_rate, init_grad = K["kgrad"](
        seg, all_maps, all_maps, all_grads, key_rows, rate_rows, errors, states, vv,
        b_part, lam_part, step_maps, step_grads,
    )
    d_rate_pre = (d_rate * rate_scale * rate_sig * (1.0 - rate_sig)).astype(BF)
    scale_part = jnp.sum(d_rate * rate_sig, axis=0)
    rate_bias_part = jnp.sum(d_rate_pre.astype(F32), axis=0)
    gate_grad = dot(group_in.T, d_gate_pre)
    query_grad = dot(group_in.T, d_query)
    key_grad = dot(group_in.T, d_key)
    value_grad = dot(group_in.T, d_value)
    rate_weight_part = dot(group_in.T, d_rate_pre)
    total = dot(d_query, query_weight.T)
    total = total + dot(d_key, key_weight.T)
    total = total + dot(d_value, value_weight.T)
    total = total + dot(d_gate_pre, gate_weight.T)
    d_normed = lax.psum_scatter(
        (total + dot(d_rate_pre, rate_weight.T)).astype(BF), "head", scatter_dimension=0, tiled=True
    ).astype(F32)
    scaled_in = d_normed * norm1_gain
    norm1_part = jnp.sum(d_normed * unit_in, axis=0)
    input_grad = d_middle + scale_in * (
        scaled_in - unit_in * jnp.mean(scaled_in * unit_in, axis=-1, keepdims=True)
    )
    mid_in = (out_weight_grad.astype(BF), gate_grad.astype(BF), d_query)
    mid_in, mlp_sums = lax.optimization_barrier((mid_in, mlp_sums))
    mid_sums = lax.psum(mid_in[:2], "seq")
    late_in = (query_grad.astype(BF), key_grad.astype(BF), value_grad.astype(BF))
    late_in, mid_sums = lax.optimization_barrier((late_in, mid_sums))
    late_sums = lax.psum(late_in, "seq")
    small = lax.psum(
        (rate_weight_part, rate_bias_part, scale_part, post_gain_part, post_bias_part), "seq"
    )
    gain_grads = lax.psum((norm1_part, norm2_part), ("seq", "head"))
    up = lambda x: x.astype(F32)
    return (
        block_out,
        input_grad,
        gain_grads[0],
        up(late_sums[0]),
        up(late_sums[1]),
        up(late_sums[2]),
        up(mid_sums[1]),
        small[0],
        small[1],
        small[2],
        init_grad[:, :head_width, :head_width],
        init_grad[:, head_width, :head_width],
        small[3],
        small[4],
        up(mid_sums[0]),
        gain_grads[1],
        up(mlp_sums[1]),
        up(mlp_sums[2]),
        up(mlp_sums[0]),
    )


def solution(mesh):
    in_specs = (
        P(("seq", "head"), None),
        P(),
        P(None, "head"),
        P(None, "head"),
        P(None, "head"),
        P(None, "head"),
        P(None, "head"),
        P("head"),
        P("head"),
        P("head", None, None),
        P("head", None),
        P("head"),
        P("head"),
        P("head", None),
        P(),
        P(None, "head"),
        P(None, "head"),
        P("head", None),
        P(("seq", "head"), None),
    )
    out_specs = (
        P(("seq", "head"), None),
        P(("seq", "head"), None),
        P(),
        P(None, "head"),
        P(None, "head"),
        P(None, "head"),
        P(None, "head"),
        P(None, "head"),
        P("head"),
        P("head"),
        P("head", None, None),
        P("head", None),
        P("head"),
        P("head"),
        P("head", None),
        P(),
        P(None, "head"),
        P(None, "head"),
        P("head", None),
    )
    return jax.shard_map(body, mesh=mesh, in_specs=in_specs, out_specs=out_specs, check_vma=False)
```

```python
import functools
import jax, jax.numpy as jnp
from jax import lax
from jax.experimental import pallas as pl
from jax.experimental.pallas import tpu as pltpu
from jax.sharding import PartitionSpec as P

CHUNK=128
MB=16
F32=jnp.float32; BF=jnp.bfloat16
LN=128
HW=64
VL=48*1024*1024

def mm(a,b,ca,cb):
    return lax.dot_general(a.astype(BF),b.astype(BF),(((ca,),(cb,)),((),())),preferred_element_type=F32)
def nn(a,b): return mm(a,b,1,0)
def nt(a,b): return mm(a,b,1,1)
def tn(a,b): return mm(a,b,0,0)
def split(a):
    hi=a.astype(BF)
    return hi,(a-hi.astype(F32)).astype(BF)
def nn3(a,b):
    ah,al=a; bh,bl=b
    return nn(ah,bh)+(nn(ah,bl)+nn(al,bh))

def lanes(shape): return lax.broadcasted_iota(jnp.int32,shape,1)
def rows(shape): return lax.broadcasted_iota(jnp.int32,shape,0)
def head_of(x,odd):
    y=pltpu.roll(x,HW,1) if odd else x
    return jnp.where(lanes(x.shape)<HW,y,0.0)
def aug(x): return jnp.where(lanes(x.shape)==HW,1.0,x)
def pair(a,b):
    return jnp.where(lanes(a.shape)<HW,a,pltpu.roll(b,HW,1))
def column(block,h):
    return jnp.sum(jnp.where(lanes(block.shape)==h,block,0.0),axis=1,keepdims=True)
def causal(C): return rows((C,C))>=lanes((C,C))
def earlier(C): return (rows((C,C))//MB)>(lanes((C,C))//MB)
def level(C,size):
    i=rows((C,C)); j=lanes((C,C))
    return (i//(2*size)==j//(2*size))&((i//size)%2==1)&((j//size)%2==0)

def block_inverse(low,C):
    eye=jnp.where(rows((C,C))==lanes((C,C)),1.0,0.0)
    size=MB
    t=eye-jnp.where(level(C,size),low,0.0)
    size*=2
    while size<C:
        part=split(jnp.where(level(C,size),low,0.0))
        ts=split(t)
        t=t-nn3(split(nn3(ts,part)),ts)
        size*=2
    return t

def map_kernel(C,k_ref,v_ref,r_ref,t_ref,uw_ref,x_ref,y_ref):
    p=pl.program_id(0)
    N=k_ref.shape[0]
    last=y_ref.shape[0]-1
    @pl.when(p==0)
    def _(): y_ref[last]=jnp.zeros((80,LN),BF)
    for odd in range(2):
        h=2*p+odd
        total=None
        for c in range(N//C):
            sl=pl.ds(c*C,C)
            k=head_of(k_ref[sl,:],odd)
            w=head_of(v_ref[sl,:],odd)-k
            ka=aug(k)
            r=column(r_ref[sl,:],h)
            kr=ka*r
            t=block_inverse(jnp.where(earlier(C),nt(ka,kr),0.0),C)
            t_ref[odd,c]=t.astype(BF)
            uw=nn(t,jnp.concatenate([ka,w],axis=1))
            uw_ref[odd,sl,:]=uw.astype(BF)
            xc=tn(kr,jnp.where(lanes(uw.shape)<LN,-uw,uw))
            x_ref[odd,c]=xc.astype(BF)
            total=xc if total is None else total+xc+nn(xc[:,:LN],total)
        a=total[:,:LN]; o=total[:,LN:]
        y_ref[h]=pair(a,o)[:80].astype(BF)
        col=jnp.sum(jnp.where(lanes(a.shape)==HW,a,0.0),axis=1,keepdims=True)[:80]
        y_ref[last]=jnp.where(lanes((80,LN))==h,col,y_ref[last].astype(F32)).astype(BF)

def local_kernel(C,q_ref,k_ref,r_ref,t_ref,uw_ref,qe_ref,zo_ref,pt_ref,vv_ref):
    p=pl.program_id(0)
    N=q_ref.shape[0]
    for c in range(N//C):
        sl=pl.ds(c*C,C)
        offs=[]
        for odd in range(2):
            h=2*p+odd
            q=head_of(q_ref[sl,:],odd); qa=aug(q)
            ka=aug(head_of(k_ref[sl,:],odd))
            kr=ka*column(r_ref[sl,:],h)
            pm=jnp.where(causal(C),nt(qa,kr),0.0)
            t=t_ref[odd,c]
            puw=nn(pm,uw_ref[odd,sl,:])
            qe_ref[odd,sl,:]=(qa-puw[:,:LN]).astype(BF)
            offs.append(q+puw[:,LN:])
            pt_ref[odd,c]=nn(pm,t).astype(BF)
            vv_ref[odd,sl,:]=tn(t,kr).astype(BF)
        zo_ref[sl,:]=pair(offs[0],offs[1])

def unpack(y,yb,h):
    y=y.astype(F32)
    col=column(yb.astype(F32),h)
    ln=lanes(y.shape)
    a=jnp.where(ln<HW,y,jnp.where(ln==HW,col,0.0))
    o=jnp.where(ln<HW,pltpu.roll(y,HW,1),0.0)
    pad=jnp.zeros((LN-80,LN),F32)
    return jnp.concatenate([a,pad],0),jnp.concatenate([o,pad],0)

def start_of(is_ref,ib_ref,odd):
    s=jnp.concatenate([is_ref[odd],ib_ref[odd],jnp.zeros((LN-HW-1,HW),F32)],axis=0)
    return jnp.concatenate([s,jnp.zeros_like(s)],axis=1)

def forward_kernel(C,seg_ref,y_ref,yb_ref,is_ref,ib_ref,x_ref,uw_ref,qe_ref,zo_ref,z_ref,e_ref,s_ref):
    p=pl.program_id(0)
    N=zo_ref.shape[0]
    segs=y_ref.shape[0]
    seg=seg_ref[0]
    add=[[None]*(N//C) for _ in range(2)]
    for odd in range(2):
        h=2*p+odd
        s=start_of(is_ref,ib_ref,odd)
        for j in range(segs-1):
            at=seg_ref[1+j]
            a,o=unpack(y_ref[at,odd],yb_ref[at,0],h)
            s=s+jnp.where(j<seg,1.0,0.0)*(nn(a,s)+o)
        for c in range(N//C):
            sl=pl.ds(c*C,C)
            sb=s.astype(BF)
            s_ref[odd,c]=sb
            uw=uw_ref[odd,sl,:]
            e_ref[odd,sl,:]=(nn(uw[:,:LN],sb)-uw[:,LN:].astype(F32)).astype(BF)
            add[odd][c]=nn(qe_ref[odd,sl,:],sb)
            x=x_ref[odd,c]
            s=s+nn(x[:,:LN],sb)+x[:,LN:].astype(F32)
    for c in range(N//C):
        sl=pl.ds(c*C,C)
        z_ref[sl,:]=zo_ref[sl,:]+pair(add[0][c],add[1][c])

def state_grad_kernel(C,dz_ref,qe_ref,x_ref,d_ref,dseg_ref):
    N=dz_ref.shape[0]
    outs=[]
    for odd in range(2):
        g=jnp.zeros((LN,LN),F32)
        for c in reversed(range(N//C)):
            sl=pl.ds(c*C,C)
            dz=head_of(dz_ref[sl,:],odd)
            d=tn(qe_ref[odd,sl,:],dz)
            d_ref[odd,c]=d
            g=g+tn(x_ref[odd,c][:,:LN],g)+d
        outs.append(g)
    dseg_ref[0]=pair(outs[0],outs[1])[:80].astype(BF)

def query_grad_kernel(C,q_ref,k_ref,r_ref,dz_ref,e_ref,s_ref,pt_ref,dq_ref,b_ref,l_ref):
    p=pl.program_id(0)
    N=q_ref.shape[0]
    for c in range(N//C):
        sl=pl.ds(c*C,C)
        outs=[]
        for odd in range(2):
            h=2*p+odd
            dz=head_of(dz_ref[sl,:],odd); dzb=dz.astype(BF)
            qa=aug(head_of(q_ref[sl,:],odd))
            ka=aug(head_of(k_ref[sl,:],odd))
            kr=ka*column(r_ref[sl,:],h)
            fu=jnp.where(causal(C),-nt(dzb,e_ref[odd,sl,:]),0.0).astype(BF)
            outs.append(dz+nt(dzb,s_ref[odd,c])+nn(fu,kr))
            b_ref[odd,sl,:]=tn(fu,qa).astype(BF)
            l_ref[odd,sl,:]=-tn(pt_ref[odd,c],dzb)
        dq_ref[sl,:]=pair(outs[0],outs[1]).astype(BF)

def key_grad_kernel(C,seg_ref,y_ref,yb_ref,da_ref,k_ref,r_ref,e_ref,s_ref,vv_ref,b_ref,l_ref,x_ref,d_ref,dq_ref,dg_ref,dk_ref,dv_ref,dr_ref,gi_ref,pk_ref):
    p=pl.program_id(0)
    N=k_ref.shape[0]
    segs=y_ref.shape[0]
    seg=seg_ref[0]
    @pl.when(p==0)
    def _(): dr_ref[...]=jnp.zeros_like(dr_ref)
    pad=jnp.zeros((LN-80,LN),F32)
    dks=[[None]*(N//C) for _ in range(2)]
    lams=[[None]*(N//C) for _ in range(2)]
    for odd in range(2):
        h=2*p+odd
        full=jnp.zeros((LN,LN),F32)
        g=jnp.zeros((LN,LN),F32)
        for j in reversed(range(segs)):
            at=seg_ref[1+j]
            a,_=unpack(y_ref[at,odd],yb_ref[at,0],h)
            d=jnp.concatenate([head_of(da_ref[at,0].astype(F32),odd),pad],0)
            full=full+tn(a,full)+d
            g=jnp.where(j==seg+1,full,g)
        gi_ref[odd]=full[:72]
        for c in reversed(range(N//C)):
            sl=pl.ds(c*C,C)
            gb=g.astype(BF)
            ka=aug(head_of(k_ref[sl,:],odd))
            r=column(r_ref[sl,:],h)
            kr=ka*r
            e=e_ref[odd,sl,:]
            lam=l_ref[odd,sl,:]-nn(vv_ref[odd,sl,:],gb)
            lb=lam.astype(BF)
            hu=jnp.where(earlier(C),-nt(lb,e),0.0).astype(BF)
            b=b_ref[odd,sl,:].astype(F32)+tn(hu,ka)-nt(e,gb)
            dks[odd][c]=r*b+nt(lb,s_ref[odd,c])+nn(hu,kr)+lam
            lams[odd][c]=lam
            dr=jnp.sum(ka*b,axis=1,keepdims=True)
            dr_ref[sl,:]=jnp.where(lanes((C,dr_ref.shape[1]))==h,dr,dr_ref[sl,:])
            g=g+tn(x_ref[odd,c][:,:LN],gb)+d_ref[odd,c]
    for c in range(N//C):
        sl=pl.ds(c*C,C)
        dk_ref[sl,:]=pair(dks[0][c],dks[1][c]).astype(BF)
        dv_ref[sl,:]=-pair(lams[0][c],lams[1][c]).astype(BF)
        dq=dq_ref[sl,:].astype(F32); dg=dg_ref[sl,:].astype(F32)
        for odd in range(2):
            first=pair(head_of(dq,odd),dks[odd][c]); second=pair(-lams[odd][c],head_of(dg,odd))
            pk_ref[odd,sl,:]=jnp.concatenate([first,second],axis=1).astype(BF)

def params(): return pltpu.CompilerParams(dimension_semantics=("arbitrary",),vmem_limit_bytes=VL)
def S(shape,dt): return jax.ShapeDtypeStruct(shape,dt)

def specs(N,hl,C):
    nc=N//C
    d={}
    d["row"]=pl.BlockSpec((N,LN),lambda p,*_:(0,p))
    d["rate"]=pl.BlockSpec((N,hl),lambda p,*_:(0,0))
    d["cc"]=pl.BlockSpec((2,nc,C,C),lambda p,*_:(p,0,0,0))
    d["n256"]=pl.BlockSpec((2,N,2*LN),lambda p,*_:(p,0,0))
    d["n128"]=pl.BlockSpec((2,N,LN),lambda p,*_:(p,0,0))
    d["x"]=pl.BlockSpec((2,nc,LN,2*LN),lambda p,*_:(p,0,0,0))
    d["s"]=pl.BlockSpec((2,nc,LN,LN),lambda p,*_:(p,0,0,0))
    d["y"]=pl.BlockSpec((hl+1,80,LN),lambda p,*_:(0,0,0))
    return d

def build(N,hl,segs,C=128):
    nc=N//C; sp=specs(N,hl,C); G=(hl//2,)
    w=hl*HW
    K={}
    K["map"]=pl.pallas_call(functools.partial(map_kernel,C),grid=G,in_specs=[sp["row"],sp["row"],sp["rate"]],
        out_specs=[sp["cc"],sp["n256"],sp["x"],sp["y"]],
        out_shape=[S((hl,nc,C,C),BF),S((hl,N,2*LN),BF),S((hl,nc,LN,2*LN),BF),S((hl+1,80,LN),BF)],compiler_params=params(),name="segment_maps")
    K["local"]=pl.pallas_call(functools.partial(local_kernel,C),grid=G,in_specs=[sp["row"],sp["row"],sp["rate"],sp["cc"],sp["n256"]],
        out_specs=[sp["n128"],sp["row"],sp["cc"],sp["n128"]],
        out_shape=[S((hl,N,LN),BF),S((N,w),F32),S((hl,nc,C,C),BF),S((hl,N,LN),BF)],compiler_params=params(),name="local_parts")
    yall=pl.BlockSpec((segs,2,80,LN),lambda p,*_:(0,p,0,0)); yball=pl.BlockSpec((segs,1,80,LN),lambda p,*_:(0,hl,0,0))
    dall=pl.BlockSpec((segs,1,80,LN),lambda p,*_:(0,p,0,0))
    ist=pl.BlockSpec((2,HW,HW),lambda p,*_:(p,0,0)); ibs=pl.BlockSpec((2,1,HW),lambda p,*_:(p,0,0))
    def gs(i,o): return pltpu.PrefetchScalarGridSpec(num_scalar_prefetch=1,grid=G,in_specs=i,out_specs=o)
    K["forward"]=pl.pallas_call(functools.partial(forward_kernel,C),grid_spec=gs([yall,yball,ist,ibs,sp["x"],sp["n256"],sp["n128"],sp["row"]],[sp["row"],sp["n128"],sp["s"]]),
        out_shape=[S((N,w),F32),S((hl,N,LN),BF),S((hl,nc,LN,LN),BF)],compiler_params=params(),name="forward_states")
    K["sgrad"]=pl.pallas_call(functools.partial(state_grad_kernel,C),grid=G,in_specs=[sp["row"],sp["n128"],sp["x"]],
        out_specs=[sp["s"],pl.BlockSpec((1,80,LN),lambda p:(p,0,0))],out_shape=[S((hl,nc,LN,LN),F32),S((hl//2,80,LN),BF)],compiler_params=params(),name="state_grads")
    K["qgrad"]=pl.pallas_call(functools.partial(query_grad_kernel,C),grid=G,in_specs=[sp["row"],sp["row"],sp["rate"],sp["row"],sp["n128"],sp["s"],sp["cc"]],
        out_specs=[sp["row"],sp["n128"],sp["n128"]],out_shape=[S((N,w),BF),S((hl,N,LN),BF),S((hl,N,LN),F32)],compiler_params=params(),name="query_grads")
    K["kgrad"]=pl.pallas_call(functools.partial(key_grad_kernel,C),grid_spec=gs([yall,yball,dall,sp["row"],sp["rate"],sp["n128"],sp["s"],sp["n128"],sp["n128"],sp["n128"],sp["x"],sp["s"],sp["row"],sp["row"]],
        [sp["row"],sp["row"],sp["rate"],pl.BlockSpec((2,72,LN),lambda p,*_:(p,0,0)),sp["n256"]]),
        out_shape=[S((N,w),BF),S((N,w),BF),S((N,hl),F32),S((hl,72,LN),F32),S((hl,N,2*LN),BF)],compiler_params=params(),name="key_grads")
    return K


EPSILON = 1e-06


def grid_of():
    seq = lax.axis_size("seq")
    x = max(lax.axis_size("head") // 2, 1)
    if seq % x:
        x = 1
    return seq // x, x


def shift(v, dz, dx):
    Z, X = grid_of()
    pairs = [(z * X + x, ((z + dz) % Z) * X + (x + dx) % X) for z in range(Z) for x in range(X)]
    return lax.ppermute(v, "seq", pairs)


def seq_gather(v):
    Z, X = grid_of()
    i = lax.axis_index("seq")
    j = jnp.arange(Z * X, dtype=jnp.int32)
    if (Z, X) != (4, 2):
        return lax.all_gather(v, "seq", axis=0, tiled=False), j
    both = jnp.stack([v, shift(v, 0, 1)])
    left = shift(both, 1, 0)
    right = shift(both, 3, 0)
    far0 = shift(left[:1], 1, 0)
    far1 = shift(right[1:], 3, 0)
    z, x = i // X, i % X
    order = ((j // X - z) % Z) * X + (j % X - x) % X
    return jnp.concatenate([both, right, far0, far1, left]), order


def head_shift(v, dy, dc):
    H = lax.axis_size("head")
    Y = H // 2
    pairs = [(y * 2 + c, ((y + dy) % Y) * 2 + (c + dc) % 2) for y in range(Y) for c in range(2)]
    return lax.ppermute(v, "head", pairs)


def head_gather(v):
    H = lax.axis_size("head")
    if H != 4:
        return lax.all_gather(v, "head", axis=0, tiled=True)
    i = lax.axis_index("head")
    y, c = i // 2, i % 2
    mine = jnp.stack([v, head_shift(v, 1, 0)])
    other = head_shift(mine, 0, 1)
    a = jnp.where(c == 0, mine, other)
    b = jnp.where(c == 0, other, mine)
    rows = [jnp.where(y == 0, a[0], a[1]), jnp.where(y == 0, b[0], b[1])]
    rows += [jnp.where(y == 0, a[1], a[0]), jnp.where(y == 0, b[1], b[0])]
    return jnp.concatenate(rows, axis=0)


def head_scatter(v):
    H = lax.axis_size("head")
    v = v.astype(BF)
    if H != 4:
        return lax.psum_scatter(v, "head", scatter_dimension=0, tiled=True).astype(F32)
    i = lax.axis_index("head")
    y, c = i // 2, i % 2
    v = v.reshape(2, 2, v.shape[0] // 4, v.shape[1])
    got = head_shift(jnp.where(c == 0, v[:, 1], v[:, 0]), 0, 1)
    half = (jnp.where(c == 0, v[:, 0], v[:, 1]).astype(F32) + got.astype(F32)).astype(BF)
    back = head_shift(jnp.where(y == 0, half[1], half[0]), 1, 0)
    return jnp.where(y == 0, half[0], half[1]).astype(F32) + back.astype(F32)


def gelu_tanh(values):
    return jax.nn.gelu(values, approximate=True)


def dot(a, b, ca=1, cb=0):
    return lax.dot_general(a, b, (((ca,), (cb,)), ((), ())), preferred_element_type=F32)


def at(v, i, axis=0):
    return lax.dynamic_index_in_dim(v, i, axis, keepdims=False)


def plus(a, b):
    return (a.astype(F32) + b.astype(F32)).astype(BF)


def pair_reduce(v):
    x = lax.axis_index("seq") % 2
    return plus(at(v, x, 1), shift(at(v, 1 - x, 1), 0, 1))


def ring_start(v):
    z = lax.axis_index("seq") // 2
    v = v.reshape((4, -1) + v.shape[1:])
    if v.shape[1] == 1:
        h = v.shape[2] // 32 * 16
        top, low = v[:, 0, :h], v[:, 0, h:]
    else:
        top, low = v[:, 0], v[:, 1]
    a = shift(at(top, (z + 2) % 4), 1, 0)
    b = shift(at(low, (z + 2) % 4), 3, 0)
    return top, low, a, b


def ring_end(state, parts):
    top, low, a, b = state
    z = lax.axis_index("seq") // 2
    join = jnp.stack if parts == 2 else lambda p: jnp.concatenate(p, axis=0)
    up = join([plus(at(top, (z + 1) % 4), a), at(low, (z + 1) % 4)])
    down = join([at(top, (z + 3) % 4), plus(at(low, (z + 3) % 4), b)])
    got = shift(up, 1, 0).astype(F32) + shift(down, 3, 0).astype(F32)
    return (join([at(top, z), at(low, z)]).astype(F32) + got).astype(BF)


def split_columns(D):
    return D * 7 // 16 // LN * LN


def result_gather(vc, vd):
    Z, X = grid_of()
    i = lax.axis_index("seq")
    z, x = i // X, i % X
    h = vc.shape[0] // 32 * 16
    left, right = shift(vc, 1, 0), shift(vc, 3, 0)
    both = jnp.stack([vd, shift(vd, 0, 1)])
    far = jnp.concatenate([shift(left[:h], 1, 0), shift(right[h:], 3, 0)], axis=0)
    mine = jnp.stack([vc, right, far, left])
    dl, dr = shift(both, 1, 0), shift(both, 3, 0)
    other = shift(mine, 0, 1)
    f0, f1 = shift(dl[:1], 1, 0), shift(dr[1:], 3, 0)
    k = jnp.arange(4, dtype=jnp.int32)
    zs = (z + k) % 4
    at_c = jnp.concatenate([zs * 2 + x, zs * 2 + 1 - x])
    at_d = jnp.stack([zs * 2 + x, zs * 2 + 1 - x], axis=1).reshape(8)
    return [mine, other], [both, dr, f0, f1, dl], jnp.concatenate([at_c, at_d]).astype(jnp.int32)


def pieces_of(refs):
    return [(ref, k) for ref in refs for k in range(ref.shape[0])]


def finish_kernel(nc, nd, plan, at_ref, *refs):
    i = pl.program_id(0)
    outs, scratch = refs[nc + nd : -1], refs[-1]

    def write(group, base):
        for out, (first, rows, turned) in zip(outs, plan):
            for slot, (ref, k) in enumerate(pieces_of(group)):
                start = pl.multiple_of(at_ref[base + slot] * rows, 16)
                scratch[pl.ds(start, rows), :] = ref[k, pl.ds(first, rows), :].astype(F32)
            if turned:
                out[...] = scratch[pl.ds(0, out.shape[1]), :].T
            else:
                out[...] = scratch[pl.ds(0, out.shape[0]), :]

    split = pl.num_programs(0) * 7 // 16

    @pl.when(i < split)
    def _():
        write(refs[:nc], 0)

    @pl.when(i >= split)
    def _():
        write(refs[nc : nc + nd], 8)


def finish(gathered, plan, widths):
    group_c, group_d, slots = gathered
    D = group_c[0].shape[2] + group_d[0].shape[2]
    rc, rd = group_c[0].shape[1], group_d[0].shape[1]
    split = group_c[0].shape[2] // LN
    in_specs = [
        pl.BlockSpec((g.shape[0], rc, LN), lambda i, o: (0, 0, jnp.minimum(i, split - 1)))
        for g in group_c
    ] + [
        pl.BlockSpec((g.shape[0], rd, LN), lambda i, o: (0, 0, jnp.maximum(i - split, 0)))
        for g in group_d
    ]
    out_specs, out_shape = [], []
    for w, (_, _, turned) in zip(widths, plan):
        if turned:
            out_specs.append(pl.BlockSpec((LN, w), lambda i, o: (i, 0)))
            out_shape.append(jax.ShapeDtypeStruct((D, w), F32))
        else:
            out_specs.append(pl.BlockSpec((w, LN), lambda i, o: (0, i)))
            out_shape.append(jax.ShapeDtypeStruct((w, D), F32))
    return pl.pallas_call(
        functools.partial(finish_kernel, len(group_c), len(group_d), plan),
        grid_spec=pltpu.PrefetchScalarGridSpec(
            num_scalar_prefetch=1,
            grid=(D // LN,),
            in_specs=in_specs,
            out_specs=out_specs,
            scratch_shapes=[pltpu.VMEM((8 * max(p[1] for p in plan), LN), F32)],
        ),
        out_shape=out_shape,
        compiler_params=params(),
        name="finish",
    )(slots, *group_c, *group_d)


def halves(v):
    hi = v.astype(BF)
    return jnp.stack([hi, (v - hi.astype(F32)).astype(BF)])


def together(*values):
    return lax.optimization_barrier(values)


def body(
    block_input,
    norm1_gain,
    query_weight,
    key_weight,
    value_weight,
    gate_weight,
    rate_weight,
    rate_bias,
    rate_scale,
    init_state,
    init_bias,
    post_gain,
    post_bias,
    out_weight,
    norm2_gain,
    mlp_gate,
    mlp_up,
    mlp_down,
    out_cotangent,
):
    local_heads = init_state.shape[0]
    model_width = block_input.shape[1]
    width = mlp_gate.shape[1]
    segs = lax.axis_size("seq")
    heads = lax.axis_size("head")
    tokens = block_input.shape[0] * heads
    K = build(tokens, local_heads, segs, CHUNK)
    seg = lax.axis_index("seq").astype(jnp.int32).reshape(1)
    wide = local_heads == segs and tokens * segs * model_width <= 1 << 23 and grid_of() == (4, 2)
    everywhere = ("seq", "head")

    input_f32 = block_input.astype(F32)
    scale_in = lax.rsqrt(jnp.mean(input_f32 * input_f32, axis=-1, keepdims=True) + EPSILON)
    unit_in = input_f32 * scale_in
    normed = (unit_in * norm1_gain).astype(BF)
    group_in = head_gather(normed)
    group_cot = head_gather(out_cotangent)
    if wide:
        normed_all = lax.all_gather(normed, everywhere, axis=0, tiled=True)
    key_rows = dot(group_in, key_weight)
    value_rows = dot(group_in, value_weight)
    rate_pre = dot(group_in, rate_weight) + rate_bias
    rate_sig = jax.nn.sigmoid(rate_pre)
    rate_rows = rate_sig * rate_scale
    inv, uw, step_maps, seg_map = K["map"](key_rows, value_rows, rate_rows)
    all_maps, order = seq_gather(seg_map)
    place = jnp.concatenate([seg, order])
    query_rows = dot(group_in, query_weight)
    gate_pre = dot(group_in, gate_weight)
    q_eff, z_off, pt, vv = K["local"](query_rows, key_rows, rate_rows, inv, uw)
    z_rows, errors, states = K["forward"](
        place, all_maps, all_maps, init_state, init_bias[:, None, :], step_maps, uw, q_eff, z_off
    )
    stat_sums = lax.psum((jnp.sum(z_rows, axis=-1), jnp.sum(z_rows * z_rows, axis=-1)), "head")
    row_mean = stat_sums[0] / model_width
    row_var = stat_sums[1] / model_width - row_mean * row_mean
    inv_scale = lax.rsqrt(row_var + EPSILON)[:, None]
    z_hat = (z_rows - row_mean[:, None]) * inv_scale
    post_out = z_hat * post_gain + post_bias
    gate_act, gelu_back = jax.vjp(gelu_tanh, gate_pre)
    gated_out = (gate_act * post_out).astype(BF)
    middle = input_f32 + head_scatter(dot(gated_out, out_weight))
    scale_mid = lax.rsqrt(jnp.mean(middle * middle, axis=-1, keepdims=True) + EPSILON)
    unit_mid = middle * scale_mid
    mlp_input = (unit_mid * norm2_gain).astype(BF)
    mlp_group = head_gather(mlp_input)
    gate_mlp = dot(mlp_gate, mlp_group, 0, 1)
    up_mlp = dot(mlp_up, mlp_group, 0, 1)
    silu_gate, silu_back = jax.vjp(jax.nn.silu, gate_mlp)
    hidden = (silu_gate * up_mlp).astype(BF)
    d_hidden = dot(mlp_down, group_cot, 1, 1)
    d_gate_mlp = silu_back(d_hidden * up_mlp)[0].astype(BF)
    d_up_mlp = (d_hidden * silu_gate).astype(BF)
    if wide:
        rows = -(-width // (16 * segs)) * 16
        fit = lambda v: jnp.pad(v, ((0, rows * segs - width), (0, 0))).reshape(segs, rows, tokens)
        by_shard = lambda v: v.reshape(segs, -1, v.shape[1])
        both = jnp.concatenate([fit(d_gate_mlp), fit(d_up_mlp)], axis=1).reshape(-1, tokens)
        last = fit(hidden).reshape(-1, tokens)
        c = split_columns(model_width)
        parts = [
            jnp.concatenate(
                [by_shard(dot(both, mlp_group[:, s]).astype(BF)), by_shard(dot(last, group_cot[:, s]).astype(BF))],
                axis=1,
            )
            for s in (slice(0, c), slice(c, None))
        ]
        d_gate_mlp, parts[0] = together(d_gate_mlp, parts[0])
        cross = pair_reduce(parts[0].reshape(4, 2, -1, c))
        near = ring_start(parts[1])
    d_mlp_input = head_scatter(dot(d_gate_mlp, mlp_gate, 0, 1) + dot(d_up_mlp, mlp_up, 0, 1))
    scaled_mid = d_mlp_input * norm2_gain
    norm2_part = jnp.sum(d_mlp_input * unit_mid, axis=0)
    d_middle = out_cotangent.astype(F32) + scale_mid * (
        scaled_mid - unit_mid * jnp.mean(scaled_mid * unit_mid, axis=-1, keepdims=True)
    )
    d_attn = d_middle.astype(BF)
    d_attn_group = head_gather(d_attn)
    d_gated = dot(d_attn_group, out_weight, 1, 1)
    out_weight_grad = dot(gated_out, d_attn_group, 0, 0).astype(BF)
    d_post = d_gated * gate_act
    d_gate_pre = gelu_back(d_gated * post_out)[0].astype(BF)
    post_gain_part = jnp.sum(d_post * z_hat, axis=0)
    post_bias_part = jnp.sum(d_post, axis=0)
    d_zhat = d_post * post_gain
    back_sums = lax.psum((jnp.sum(d_zhat, axis=-1), jnp.sum(d_zhat * z_hat, axis=-1)), "head")
    d_z = inv_scale * (
        d_zhat - back_sums[0][:, None] / model_width - z_hat * (back_sums[1][:, None] / model_width)
    )
    step_grads, seg_grad = K["sgrad"](d_z, q_eff, step_maps)
    if wide:
        seg_grad, cross, near = together(seg_grad, cross, near)
    all_grads, _ = seq_gather(seg_grad)
    if wide:
        all_grads, near, out_late = together(all_grads, near, out_weight_grad)
        second = ring_end(near, 2)
        out_slice = lax.psum_scatter(out_late, "seq", scatter_dimension=0, tiled=True)
    d_query, b_part, lam_part = K["qgrad"](query_rows, key_rows, rate_rows, d_z, errors, states, pt)
    d_key, d_value, d_rate, init_grad, packed = K["kgrad"](
        place, all_maps, all_maps, all_grads, key_rows, rate_rows, errors, states, vv,
        b_part, lam_part, step_maps, step_grads, d_query, d_gate_pre,
    )
    if wide:
        d_rate, packed, second = together(d_rate, packed, second)
        second = pair_reduce(second[None])[0]
        first = ring_end(ring_start(cross), 1)
    d_rate_pre = (d_rate * rate_scale * rate_sig * (1.0 - rate_sig)).astype(BF)
    scale_part = jnp.sum(d_rate * rate_sig, axis=0)
    total = dot(d_query, query_weight, 1, 1)
    total = total + dot(d_key, key_weight, 1, 1)
    total = total + dot(d_value, value_weight, 1, 1)
    total = total + dot(d_gate_pre, gate_weight, 1, 1)
    d_normed = head_scatter(total + dot(d_rate_pre, rate_weight, 1, 1))
    scaled_in = d_normed * norm1_gain
    norm1_part = jnp.sum(d_normed * unit_in, axis=0)
    input_grad = d_middle + scale_in * (
        scaled_in - unit_in * jnp.mean(scaled_in * unit_in, axis=-1, keepdims=True)
    )
    block_out = (middle + head_scatter(dot(hidden, mlp_down, 0, 0))).astype(BF)

    if wide:
        packed = lax.all_to_all(packed, "seq", split_axis=0, concat_axis=0, tiled=True)
        packed = packed.reshape(segs * tokens, packed.shape[2])
        own = [dot(packed, v, 0, 0).astype(BF) for v in (normed_all[:, :c], normed_all[:, c:])]
        norm_parts = lax.psum((norm1_part, norm2_part), "head")
        ends = [0]
        extra = [d_rate_pre.reshape(-1)]
        for v in (scale_part, post_gain_part, post_bias_part, *norm_parts):
            extra.append(halves(v).reshape(-1))
        for v in extra:
            ends.append(ends[-1] + v.shape[0])
        cd = model_width - c
        extra = jnp.concatenate(extra + [jnp.zeros((16 * cd - ends[-1],), BF)]).reshape(16, cd)
        gathered = result_gather(
            jnp.concatenate([first, own[0], out_slice[:, :c]], axis=0),
            jnp.concatenate([second, own[1], out_slice[:, c:], extra], axis=0),
        )
        full = segs * HW
        first_row = 3 * rows
        plan = tuple((t * rows, rows, False) for t in range(3))
        plan += tuple((first_row + t * HW, HW, t < 4) for t in range(5))
        sums = finish(gathered, plan, (width,) * 3 + (full,) * 5)
        gate_sum, up_sum, down_sum, query_sum, key_sum, value_sum, pre_sum, out_sum = sums
        gate_sum, up_sum = gate_sum.T, up_sum.T
        shared = jnp.concatenate([g[:, -16:] for g in gathered[1]], axis=0).reshape(segs, -1)
        shared = shared[jnp.argsort(gathered[2][segs:])]
        from_all = [shared[:, s:e] for s, e in zip(ends[:-1], ends[1:])]
        d_rate_all = from_all[0].reshape(segs * tokens, local_heads)
        totals = [jnp.sum(v.astype(F32).reshape(2 * segs, -1), axis=0) for v in from_all[1:]]
        small = (
            dot(normed_all, d_rate_all, 0, 0),
            jnp.sum(d_rate_all.astype(F32), axis=0),
            *totals[:3],
        )
        gain_grads = totals[3:]
    else:
        grads = (
            dot(hidden, group_cot),
            dot(mlp_group, d_gate_mlp, 0, 1),
            dot(mlp_group, d_up_mlp, 0, 1),
            dot(group_in, d_query, 0, 0),
            dot(group_in, d_key, 0, 0),
            dot(group_in, d_value, 0, 0),
            dot(group_in, d_gate_pre, 0, 0),
            out_weight_grad,
        )
        sums = lax.psum(tuple(g.astype(BF) for g in grads), "seq")
        down_sum, gate_sum, up_sum, query_sum, key_sum, value_sum, pre_sum, out_sum = (
            s.astype(F32) for s in sums
        )
        small = lax.psum(
            (
                dot(group_in, d_rate_pre, 0, 0),
                jnp.sum(d_rate_pre.astype(F32), axis=0),
                scale_part,
                post_gain_part,
                post_bias_part,
            ),
            "seq",
        )
        gain_grads = lax.psum((norm1_part, norm2_part), everywhere)
    return (
        block_out,
        input_grad,
        gain_grads[0],
        query_sum,
        key_sum,
        value_sum,
        pre_sum,
        small[0],
        small[1],
        small[2],
        init_grad[:, :HW, :HW],
        init_grad[:, HW, :HW],
        small[3],
        small[4],
        out_sum,
        gain_grads[1],
        gate_sum,
        up_sum,
        down_sum,
    )


def solution(mesh):
    in_specs = (
        P(("seq", "head"), None),
        P(),
        P(None, "head"),
        P(None, "head"),
        P(None, "head"),
        P(None, "head"),
        P(None, "head"),
        P("head"),
        P("head"),
        P("head", None, None),
        P("head", None),
        P("head"),
        P("head"),
        P("head", None),
        P(),
        P(None, "head"),
        P(None, "head"),
        P("head", None),
        P(("seq", "head"), None),
    )
    out_specs = (
        P(("seq", "head"), None),
        P(("seq", "head"), None),
        P(),
        P(None, "head"),
        P(None, "head"),
        P(None, "head"),
        P(None, "head"),
        P(None, "head"),
        P("head"),
        P("head"),
        P("head", None, None),
        P("head", None),
        P("head"),
        P("head"),
        P("head", None),
        P(),
        P(None, "head"),
        P(None, "head"),
        P("head", None),
    )
    return jax.shard_map(body, mesh=mesh, in_specs=in_specs, out_specs=out_specs, check_vma=False)
```

```python
import functools
import jax, jax.numpy as jnp
from jax import lax
from jax.experimental import pallas as pl
from jax.experimental.pallas import tpu as pltpu
from jax.sharding import PartitionSpec as P

CHUNK=128
MB=16
F32=jnp.float32; BF=jnp.bfloat16
LN=128
HW=64
VL=48*1024*1024

def mm(a,b,ca,cb):
    return lax.dot_general(a.astype(BF),b.astype(BF),(((ca,),(cb,)),((),())),preferred_element_type=F32)
def nn(a,b): return mm(a,b,1,0)
def nt(a,b): return mm(a,b,1,1)
def tn(a,b): return mm(a,b,0,0)
def split(a):
    hi=a.astype(BF)
    return hi,(a-hi.astype(F32)).astype(BF)
def nn3(a,b):
    ah,al=a; bh,bl=b
    return nn(ah,bh)+(nn(ah,bl)+nn(al,bh))

def lanes(shape): return lax.broadcasted_iota(jnp.int32,shape,1)
def rows(shape): return lax.broadcasted_iota(jnp.int32,shape,0)
def head_of(x,odd):
    y=pltpu.roll(x,HW,1) if odd else x
    return jnp.where(lanes(x.shape)<HW,y,0.0)
def aug(x): return jnp.where(lanes(x.shape)==HW,1.0,x)
def pair(a,b):
    return jnp.where(lanes(a.shape)<HW,a,pltpu.roll(b,HW,1))
def column(block,h):
    return jnp.sum(jnp.where(lanes(block.shape)==h,block,0.0),axis=1,keepdims=True)
def causal(C): return rows((C,C))>=lanes((C,C))
def earlier(C): return (rows((C,C))>>4)>(lanes((C,C))>>4)
def level(C,b):
    i=rows((C,C)); j=lanes((C,C))
    return ((i>>(b+1))==(j>>(b+1)))&((i>>b)>(j>>b))

def block_inverses(lows,C):
    b=4
    mask=level(C,b)
    ys=[jnp.where(mask,-low,0.0) for low in lows]
    b+=1
    while (1<<b)<C:
        mask=level(C,b)
        parts=[jnp.where(mask,low,0.0) for low in lows]
        yb=[y.astype(BF) for y in ys]
        zs=[p+nn(y,p) for y,p in zip(yb,parts)]
        ys=[y-(z+nn(z,b2)) for y,z,b2 in zip(ys,zs,yb)]
        b+=1
    return ys

def map_kernel(C,k_ref,v_ref,r_ref,t_ref,uw_ref,x_ref,y_ref):
    p=pl.program_id(0)
    N=k_ref.shape[0]
    last=y_ref.shape[0]-1
    @pl.when(p==0)
    def _(): y_ref[last]=jnp.zeros((80,LN),BF)
    units=[(odd,c,pl.ds(c*C,C)) for c in range(N//C) for odd in range(2)]
    mask=earlier(C)
    eye=jnp.where(rows((C,C))==lanes((C,C)),1.0,0.0)
    ks=[head_of(k_ref[sl,:],odd) for odd,c,sl in units]
    kws=[jnp.concatenate([aug(k),head_of(v_ref[sl,:],odd)-k],axis=1) for k,(odd,c,sl) in zip(ks,units)]
    krs=[(kw[:,:LN]*column(r_ref[sl,:],2*p+odd)).astype(BF) for kw,(odd,c,sl) in zip(kws,units)]
    lows=[jnp.where(mask,nt(kw[:,:LN],kr),0.0) for kw,kr in zip(kws,krs)]
    ys=block_inverses(lows,C)
    total=[None,None]
    uws=[kw+nn(y,kw) for y,kw in zip(ys,kws)]
    xcs=[tn(kr,jnp.where(lanes(uw.shape)<LN,-uw,uw)) for kr,uw in zip(krs,uws)]
    for (odd,c,sl),y,uw,xc in zip(units,ys,uws,xcs):
        t_ref[odd,c]=(y+eye).astype(BF)
        uw_ref[odd,sl,:]=uw.astype(BF)
        x_ref[odd,c]=xc.astype(BF)
        total[odd]=xc if total[odd] is None else total[odd]+xc+nn(xc[:,:LN],total[odd])
    for odd in range(2):
        h=2*p+odd
        a=total[odd][:,:LN]; o=total[odd][:,LN:]
        y_ref[h]=pair(a,o)[:80].astype(BF)
        col=jnp.sum(jnp.where(lanes(a.shape)==HW,a,0.0),axis=1,keepdims=True)[:80]
        y_ref[last]=jnp.where(lanes((80,LN))==h,col,y_ref[last].astype(F32)).astype(BF)

def local_kernel(C,q_ref,k_ref,r_ref,t_ref,uw_ref,qe_ref,zo_ref,pt_ref,vv_ref):
    p=pl.program_id(0)
    N=q_ref.shape[0]
    mask=causal(C)
    for c in range(N//C):
        sl=pl.ds(c*C,C)
        offs=[]
        for odd in range(2):
            h=2*p+odd
            q=head_of(q_ref[sl,:],odd); qa=aug(q)
            ka=aug(head_of(k_ref[sl,:],odd))
            kr=ka*column(r_ref[sl,:],h)
            pm=jnp.where(mask,nt(qa,kr),0.0)
            t=t_ref[odd,c]
            puw=nn(pm,uw_ref[odd,sl,:])
            qe_ref[odd,sl,:]=(qa-puw[:,:LN]).astype(BF)
            offs.append(q+puw[:,LN:])
            pt_ref[odd,c]=nn(pm,t).astype(BF)
            vv_ref[odd,sl,:]=tn(t,kr).astype(BF)
        zo_ref[sl,:]=pair(offs[0],offs[1])

def unpack(y,yb,h):
    y=y.astype(F32)
    col=column(yb.astype(F32),h)
    ln=lanes(y.shape)
    a=jnp.where(ln<HW,y,jnp.where(ln==HW,col,0.0))
    o=jnp.where(ln<HW,pltpu.roll(y,HW,1),0.0)
    pad=jnp.zeros((LN-80,LN),F32)
    return jnp.concatenate([a,pad],0),jnp.concatenate([o,pad],0)

def start_of(is_ref,ib_ref,odd):
    s=jnp.concatenate([is_ref[odd],ib_ref[odd],jnp.zeros((LN-HW-1,HW),F32)],axis=0)
    return jnp.concatenate([s,jnp.zeros_like(s)],axis=1)

def forward_kernel(C,seg_ref,y_ref,yb_ref,is_ref,ib_ref,x_ref,uw_ref,qe_ref,zo_ref,z_ref,e_ref,s_ref):
    p=pl.program_id(0)
    N=zo_ref.shape[0]
    segs=y_ref.shape[0]
    seg=seg_ref[0]
    nc=N//C
    ss=[start_of(is_ref,ib_ref,odd) for odd in range(2)]
    for j in range(segs-1):
        at=seg_ref[1+j]
        on=jnp.where(j<seg,1.0,0.0)
        for odd in range(2):
            a,o=unpack(y_ref[at,odd],yb_ref[at,0],2*p+odd)
            ss[odd]=ss[odd]+on*(nn(a,ss[odd])+o)
    sbs=[[],[]]
    for c in range(nc):
        for odd in range(2):
            sb=ss[odd].astype(BF)
            sbs[odd].append(sb)
            x=x_ref[odd,c]
            ss[odd]=ss[odd]+nn(x[:,:LN],sb)+x[:,LN:].astype(F32)
    for c in range(nc):
        sl=pl.ds(c*C,C)
        add=[]
        for odd in range(2):
            sb=sbs[odd][c]
            s_ref[odd,c]=sb
            uw=uw_ref[odd,sl,:]
            e_ref[odd,sl,:]=(nn(uw[:,:LN],sb)-uw[:,LN:].astype(F32)).astype(BF)
            add.append(nn(qe_ref[odd,sl,:],sb))
        z_ref[sl,:]=zo_ref[sl,:]+pair(add[0],add[1])

def state_grad_kernel(C,dz_ref,qe_ref,x_ref,d_ref,dseg_ref):
    N=dz_ref.shape[0]
    outs=[]
    for odd in range(2):
        g=jnp.zeros((LN,LN),F32)
        for c in reversed(range(N//C)):
            sl=pl.ds(c*C,C)
            dz=head_of(dz_ref[sl,:],odd)
            d=tn(qe_ref[odd,sl,:],dz)
            d_ref[odd,c]=d
            g=g+tn(x_ref[odd,c][:,:LN],g)+d
        outs.append(g)
    dseg_ref[0]=pair(outs[0],outs[1])[:80].astype(BF)

def query_grad_kernel(C,q_ref,k_ref,r_ref,dz_ref,e_ref,s_ref,pt_ref,dq_ref,b_ref,l_ref):
    p=pl.program_id(0)
    N=q_ref.shape[0]
    mask=causal(C)
    for c in range(N//C):
        sl=pl.ds(c*C,C)
        outs=[]
        for odd in range(2):
            h=2*p+odd
            dz=head_of(dz_ref[sl,:],odd); dzb=dz.astype(BF)
            qa=aug(head_of(q_ref[sl,:],odd))
            ka=aug(head_of(k_ref[sl,:],odd))
            kr=ka*column(r_ref[sl,:],h)
            fu=jnp.where(mask,-nt(dzb,e_ref[odd,sl,:]),0.0).astype(BF)
            outs.append(dz+nt(dzb,s_ref[odd,c])+nn(fu,kr))
            b_ref[odd,sl,:]=tn(fu,qa).astype(BF)
            l_ref[odd,sl,:]=-tn(pt_ref[odd,c],dzb)
        dq_ref[sl,:]=pair(outs[0],outs[1]).astype(BF)

def key_grad_kernel(C,seg_ref,y_ref,yb_ref,da_ref,k_ref,r_ref,e_ref,s_ref,vv_ref,b_ref,l_ref,x_ref,d_ref,dq_ref,dg_ref,dk_ref,dv_ref,dr_ref,gi_ref,pk_ref):
    p=pl.program_id(0)
    N=k_ref.shape[0]
    segs=y_ref.shape[0]
    seg=seg_ref[0]
    @pl.when(p==0)
    def _(): dr_ref[...]=jnp.zeros_like(dr_ref)
    pad=jnp.zeros((LN-80,LN),F32)
    nc=N//C
    full=[jnp.zeros((LN,LN),F32) for _ in range(2)]
    gs=[jnp.zeros((LN,LN),F32) for _ in range(2)]
    for j in reversed(range(segs)):
        at=seg_ref[1+j]
        for odd in range(2):
            a,_=unpack(y_ref[at,odd],yb_ref[at,0],2*p+odd)
            d=jnp.concatenate([head_of(da_ref[at,0].astype(F32),odd),pad],0)
            full[odd]=full[odd]+tn(a,full[odd])+d
            gs[odd]=jnp.where(j==seg+1,full[odd],gs[odd])
    for odd in range(2): gi_ref[odd]=full[odd][:72]
    gbs=[[None]*nc for _ in range(2)]
    for c in reversed(range(nc)):
        for odd in range(2):
            gb=gs[odd].astype(BF)
            gbs[odd][c]=gb
            gs[odd]=gs[odd]+tn(x_ref[odd,c][:,:LN],gb)+d_ref[odd,c]
    mask=earlier(C)
    for c in range(nc):
        sl=pl.ds(c*C,C)
        dks=[]; lams=[]
        for odd in range(2):
            h=2*p+odd
            gb=gbs[odd][c]
            ka=aug(head_of(k_ref[sl,:],odd))
            r=column(r_ref[sl,:],h)
            kr=ka*r
            e=e_ref[odd,sl,:]
            lam=l_ref[odd,sl,:]-nn(vv_ref[odd,sl,:],gb)
            lb=lam.astype(BF)
            hu=jnp.where(mask,-nt(lb,e),0.0).astype(BF)
            b=b_ref[odd,sl,:].astype(F32)+tn(hu,ka)-nt(e,gb)
            dks.append(r*b+nt(lb,s_ref[odd,c])+nn(hu,kr)+lam)
            lams.append(lam)
            dr=jnp.sum(ka*b,axis=1,keepdims=True)
            dr_ref[sl,:]=jnp.where(lanes((C,dr_ref.shape[1]))==h,dr,dr_ref[sl,:])
        dk_ref[sl,:]=pair(dks[0],dks[1]).astype(BF)
        dv_ref[sl,:]=-pair(lams[0],lams[1]).astype(BF)
        dq=dq_ref[sl,:].astype(F32); dg=dg_ref[sl,:].astype(F32)
        for odd in range(2):
            first=pair(head_of(dq,odd),dks[odd]); second=pair(-lams[odd],head_of(dg,odd))
            pk_ref[odd,sl,:]=jnp.concatenate([first,second],axis=1).astype(BF)

def params(): return pltpu.CompilerParams(dimension_semantics=("arbitrary",),vmem_limit_bytes=VL)
def S(shape,dt): return jax.ShapeDtypeStruct(shape,dt)

def specs(N,hl,C):
    nc=N//C
    d={}
    d["row"]=pl.BlockSpec((N,LN),lambda p,*_:(0,p))
    d["rate"]=pl.BlockSpec((N,hl),lambda p,*_:(0,0))
    d["cc"]=pl.BlockSpec((2,nc,C,C),lambda p,*_:(p,0,0,0))
    d["n256"]=pl.BlockSpec((2,N,2*LN),lambda p,*_:(p,0,0))
    d["n128"]=pl.BlockSpec((2,N,LN),lambda p,*_:(p,0,0))
    d["x"]=pl.BlockSpec((2,nc,LN,2*LN),lambda p,*_:(p,0,0,0))
    d["s"]=pl.BlockSpec((2,nc,LN,LN),lambda p,*_:(p,0,0,0))
    d["y"]=pl.BlockSpec((hl+1,80,LN),lambda p,*_:(0,0,0))
    return d

def build(N,hl,segs,C=128):
    nc=N//C; sp=specs(N,hl,C); G=(hl//2,)
    w=hl*HW
    K={}
    K["map"]=pl.pallas_call(functools.partial(map_kernel,C),grid=G,in_specs=[sp["row"],sp["row"],sp["rate"]],
        out_specs=[sp["cc"],sp["n256"],sp["x"],sp["y"]],
        out_shape=[S((hl,nc,C,C),BF),S((hl,N,2*LN),BF),S((hl,nc,LN,2*LN),BF),S((hl+1,80,LN),BF)],compiler_params=params(),name="segment_maps")
    K["local"]=pl.pallas_call(functools.partial(local_kernel,C),grid=G,in_specs=[sp["row"],sp["row"],sp["rate"],sp["cc"],sp["n256"]],
        out_specs=[sp["n128"],sp["row"],sp["cc"],sp["n128"]],
        out_shape=[S((hl,N,LN),BF),S((N,w),F32),S((hl,nc,C,C),BF),S((hl,N,LN),BF)],compiler_params=params(),name="local_parts")
    yall=pl.BlockSpec((segs,2,80,LN),lambda p,*_:(0,p,0,0)); yball=pl.BlockSpec((segs,1,80,LN),lambda p,*_:(0,hl,0,0))
    dall=pl.BlockSpec((segs,1,80,LN),lambda p,*_:(0,p,0,0))
    ist=pl.BlockSpec((2,HW,HW),lambda p,*_:(p,0,0)); ibs=pl.BlockSpec((2,1,HW),lambda p,*_:(p,0,0))
    def gs(i,o): return pltpu.PrefetchScalarGridSpec(num_scalar_prefetch=1,grid=G,in_specs=i,out_specs=o)
    K["forward"]=pl.pallas_call(functools.partial(forward_kernel,C),grid_spec=gs([yall,yball,ist,ibs,sp["x"],sp["n256"],sp["n128"],sp["row"]],[sp["row"],sp["n128"],sp["s"]]),
        out_shape=[S((N,w),F32),S((hl,N,LN),BF),S((hl,nc,LN,LN),BF)],compiler_params=params(),name="forward_states")
    K["sgrad"]=pl.pallas_call(functools.partial(state_grad_kernel,C),grid=G,in_specs=[sp["row"],sp["n128"],sp["x"]],
        out_specs=[sp["s"],pl.BlockSpec((1,80,LN),lambda p:(p,0,0))],out_shape=[S((hl,nc,LN,LN),F32),S((hl//2,80,LN),BF)],compiler_params=params(),name="state_grads")
    K["qgrad"]=pl.pallas_call(functools.partial(query_grad_kernel,C),grid=G,in_specs=[sp["row"],sp["row"],sp["rate"],sp["row"],sp["n128"],sp["s"],sp["cc"]],
        out_specs=[sp["row"],sp["n128"],sp["n128"]],out_shape=[S((N,w),BF),S((hl,N,LN),BF),S((hl,N,LN),F32)],compiler_params=params(),name="query_grads")
    K["kgrad"]=pl.pallas_call(functools.partial(key_grad_kernel,C),grid_spec=gs([yall,yball,dall,sp["row"],sp["rate"],sp["n128"],sp["s"],sp["n128"],sp["n128"],sp["n128"],sp["x"],sp["s"],sp["row"],sp["row"]],
        [sp["row"],sp["row"],sp["rate"],pl.BlockSpec((2,72,LN),lambda p,*_:(p,0,0)),sp["n256"]]),
        out_shape=[S((N,w),BF),S((N,w),BF),S((N,hl),F32),S((hl,72,LN),F32),S((hl,N,2*LN),BF)],compiler_params=params(),name="key_grads")
    return K


EPSILON = 1e-06


def grid_of():
    seq = lax.axis_size("seq")
    x = max(lax.axis_size("head") // 2, 1)
    if seq % x:
        x = 1
    return seq // x, x


def shift(v, dz, dx):
    Z, X = grid_of()
    pairs = [(z * X + x, ((z + dz) % Z) * X + (x + dx) % X) for z in range(Z) for x in range(X)]
    return lax.ppermute(v, "seq", pairs)


def seq_gather(v, *later):
    Z, X = grid_of()
    i = lax.axis_index("seq")
    j = jnp.arange(Z * X, dtype=jnp.int32)
    if (Z, X) != (4, 2):
        return lax.all_gather(v, "seq", axis=0, tiled=False), j
    other = shift(v, 0, 1)
    if later:
        other, later = together(other, later)
    both = jnp.stack([v, other])
    left = shift(both, 1, 0)
    right = shift(both, 3, 0)
    far0 = shift(left[:1], 1, 0)
    far1 = shift(right[1:], 3, 0)
    z, x = i // X, i % X
    every = jnp.concatenate([both, right, far0, far1, left])
    if later:
        return every, *later
    return every, ((j // X - z) % Z) * X + (j % X - x) % X


def head_shift(v, dy, dc):
    H = lax.axis_size("head")
    Y = H // 2
    pairs = [(y * 2 + c, ((y + dy) % Y) * 2 + (c + dc) % 2) for y in range(Y) for c in range(2)]
    return lax.ppermute(v, "head", pairs)


def head_gather(v):
    H = lax.axis_size("head")
    if H != 4:
        return lax.all_gather(v, "head", axis=0, tiled=True)
    i = lax.axis_index("head")
    y, c = i // 2, i % 2
    mine = jnp.stack([v, head_shift(v, 1, 0)])
    other = head_shift(mine, 0, 1)
    a = jnp.where(c == 0, mine, other)
    b = jnp.where(c == 0, other, mine)
    rows = [jnp.where(y == 0, a[0], a[1]), jnp.where(y == 0, b[0], b[1])]
    rows += [jnp.where(y == 0, a[1], a[0]), jnp.where(y == 0, b[1], b[0])]
    return jnp.concatenate(rows, axis=0)


def head_scatter(v):
    H = lax.axis_size("head")
    v = v.astype(BF)
    if H != 4:
        return lax.psum_scatter(v, "head", scatter_dimension=0, tiled=True).astype(F32)
    i = lax.axis_index("head")
    y, c = i // 2, i % 2
    v = v.reshape(2, 2, v.shape[0] // 4, v.shape[1])
    got = head_shift(jnp.where(c == 0, v[:, 1], v[:, 0]), 0, 1)
    half = (jnp.where(c == 0, v[:, 0], v[:, 1]).astype(F32) + got.astype(F32)).astype(BF)
    back = head_shift(jnp.where(y == 0, half[1], half[0]), 1, 0)
    return jnp.where(y == 0, half[0], half[1]).astype(F32) + back.astype(F32)


def gelu_tanh(values):
    return jax.nn.gelu(values, approximate=True)


def dot(a, b, ca=1, cb=0):
    return lax.dot_general(a, b, (((ca,), (cb,)), ((), ())), preferred_element_type=F32)


def together(*values):
    return lax.optimization_barrier(values)


def at(v, i, axis=0):
    return lax.dynamic_index_in_dim(v, i, axis, keepdims=False)


def plus(a, b):
    return (a.astype(F32) + b.astype(F32)).astype(BF)


def slices_kernel(at_ref, g0, u0, h0, g1, u1, h1, x_ref, c_ref, send_ref, keep_ref):
    rows = g0.shape[0]
    for g, u, h, out in ((g0, u0, h0, send_ref), (g1, u1, h1, keep_ref)):
        for t, (left, right) in enumerate(((g, x_ref), (u, x_ref), (h, c_ref))):
            out[pl.ds(t * rows, rows), :] = dot(left[...], right[...]).astype(BF)


def mlp_slices(k, rows, d_gate, d_up, hidden, mlp_group, cot_group):
    i = lax.axis_index("seq")
    z, x = i // 2, i % 2
    to = ((z + k) % 4) * 2
    which = jnp.stack([to + 1 - x, to + x]).astype(jnp.int32)
    N, D = mlp_group.shape
    tile = min(D, 512)
    act = [pl.BlockSpec((rows, N), lambda j, o, n=n: (o[n], 0)) for n in (0, 1)]
    col = pl.BlockSpec((N, tile), lambda j, o: (0, j))
    out = pl.BlockSpec((3 * rows, tile), lambda j, o: (0, j))
    return pl.pallas_call(
        slices_kernel,
        grid_spec=pltpu.PrefetchScalarGridSpec(
            num_scalar_prefetch=1,
            grid=(D // tile,),
            in_specs=[act[0]] * 3 + [act[1]] * 3 + [col, col],
            out_specs=[out, out],
        ),
        out_shape=[jax.ShapeDtypeStruct((3 * rows, D), BF)] * 2,
        compiler_params=params(),
        name="mlp_slices",
    )(which, d_gate, d_up, hidden, d_gate, d_up, hidden, mlp_group, cot_group)


def gather1(v):
    return shift(v, 1, 0), shift(v, 0, 1)


def gather2(v, left):
    return shift(v, 3, 0), shift(left, 0, 1)


def gather3(v, left, right):
    h = v.shape[0] // 32 * 16
    return shift(left[:h], 1, 0), shift(right[h:], 3, 0), shift(right, 0, 1)


def gather4(far_a, far_b):
    far = jnp.concatenate([far_a, far_b], axis=0)
    return far, shift(far, 0, 1)


def slots():
    i = lax.axis_index("seq")
    z, x = i // 2, i % 2
    zs = (z + jnp.arange(4, dtype=jnp.int32)) % 4
    return jnp.concatenate([zs * 2 + x, zs * 2 + 1 - x]).astype(jnp.int32)


def finish_kernel(plan, at_ref, *refs):
    pieces, outs, scratch = refs[:8], refs[8:-1], refs[-1]
    for out, (first, rows, turned) in zip(outs, plan):
        for slot, ref in enumerate(pieces):
            start = pl.multiple_of(at_ref[slot] * rows, 16)
            scratch[pl.ds(start, rows), :] = ref[pl.ds(first, rows), :].astype(F32)
        if turned:
            out[...] = scratch[pl.ds(0, out.shape[1]), :].T
        else:
            out[...] = scratch[pl.ds(0, out.shape[0]), :]


def finish(pieces, plan, widths, name):
    R, D = pieces[0].shape
    out_specs, out_shape = [], []
    for w, (_, _, turned) in zip(widths, plan):
        if turned:
            out_specs.append(pl.BlockSpec((LN, w), lambda i, o: (i, 0)))
            out_shape.append(jax.ShapeDtypeStruct((D, w), F32))
        else:
            out_specs.append(pl.BlockSpec((w, LN), lambda i, o: (0, i)))
            out_shape.append(jax.ShapeDtypeStruct((w, D), F32))
    return pl.pallas_call(
        functools.partial(finish_kernel, plan),
        grid_spec=pltpu.PrefetchScalarGridSpec(
            num_scalar_prefetch=1,
            grid=(D // LN,),
            in_specs=[pl.BlockSpec((R, LN), lambda i, o: (0, i))] * 8,
            out_specs=out_specs,
            scratch_shapes=[pltpu.VMEM((8 * max(p[1] for p in plan), LN), F32)],
        ),
        out_shape=out_shape,
        compiler_params=params(),
        name=name,
    )(slots(), *pieces)


def halves(v):
    hi = v.astype(BF)
    return jnp.stack([hi, (v - hi.astype(F32)).astype(BF)])


def body(
    block_input,
    norm1_gain,
    query_weight,
    key_weight,
    value_weight,
    gate_weight,
    rate_weight,
    rate_bias,
    rate_scale,
    init_state,
    init_bias,
    post_gain,
    post_bias,
    out_weight,
    norm2_gain,
    mlp_gate,
    mlp_up,
    mlp_down,
    out_cotangent,
):
    local_heads = init_state.shape[0]
    model_width = block_input.shape[1]
    width = mlp_gate.shape[1]
    segs = lax.axis_size("seq")
    heads = lax.axis_size("head")
    tokens = block_input.shape[0] * heads
    K = build(tokens, local_heads, segs, CHUNK)
    seg = lax.axis_index("seq").astype(jnp.int32).reshape(1)
    wide = local_heads == segs and tokens * segs * model_width <= 1 << 23 and grid_of() == (4, 2)
    everywhere = ("seq", "head")

    input_f32 = block_input.astype(F32)
    scale_in = lax.rsqrt(jnp.mean(input_f32 * input_f32, axis=-1, keepdims=True) + EPSILON)
    unit_in = input_f32 * scale_in
    normed = (unit_in * norm1_gain).astype(BF)
    group_in = head_gather(normed)
    group_cot = head_gather(out_cotangent)
    key_rows = dot(group_in, key_weight)
    value_rows = dot(group_in, value_weight)
    rate_pre = dot(group_in, rate_weight) + rate_bias
    rate_sig = jax.nn.sigmoid(rate_pre)
    rate_rows = rate_sig * rate_scale
    inv, uw, step_maps, seg_map = K["map"](key_rows, value_rows, rate_rows)
    all_maps, order = seq_gather(seg_map)
    if wide:
        normed_late, all_maps = together(normed, all_maps)
        normed_all = lax.all_gather(normed_late, everywhere, axis=0, tiled=True)
    place = jnp.concatenate([seg, order])
    query_rows = dot(group_in, query_weight)
    gate_pre = dot(group_in, gate_weight)
    q_eff, z_off, pt, vv = K["local"](query_rows, key_rows, rate_rows, inv, uw)
    z_rows, errors, states = K["forward"](
        place, all_maps, all_maps, init_state, init_bias[:, None, :], step_maps, uw, q_eff, z_off
    )
    stat_sums = lax.psum((jnp.sum(z_rows, axis=-1), jnp.sum(z_rows * z_rows, axis=-1)), "head")
    row_mean = stat_sums[0] / model_width
    row_var = stat_sums[1] / model_width - row_mean * row_mean
    inv_scale = lax.rsqrt(row_var + EPSILON)[:, None]
    z_hat = (z_rows - row_mean[:, None]) * inv_scale
    post_out = z_hat * post_gain + post_bias
    gate_act, gelu_back = jax.vjp(gelu_tanh, gate_pre)
    gated_out = (gate_act * post_out).astype(BF)
    middle = input_f32 + head_scatter(dot(gated_out, out_weight))
    scale_mid = lax.rsqrt(jnp.mean(middle * middle, axis=-1, keepdims=True) + EPSILON)
    unit_mid = middle * scale_mid
    mlp_input = (unit_mid * norm2_gain).astype(BF)
    mlp_group = head_gather(mlp_input)
    gate_mlp = dot(mlp_gate, mlp_group, 0, 1)
    up_mlp = dot(mlp_up, mlp_group, 0, 1)
    silu_gate, silu_back = jax.vjp(jax.nn.silu, gate_mlp)
    hidden = (silu_gate * up_mlp).astype(BF)
    d_hidden = dot(mlp_down, group_cot, 1, 1)
    d_gate_mlp = silu_back(d_hidden * up_mlp)[0].astype(BF)
    d_up_mlp = (d_hidden * silu_gate).astype(BF)
    if wide:
        rows = -(-width // (16 * segs)) * 16
        slices = lambda k: mlp_slices(k, rows, d_gate_mlp, d_up_mlp, hidden, mlp_group, group_cot)
        d_gate_mlp, (sent, kept2) = together(d_gate_mlp, slices(2))
        got2 = shift(sent, 0, 1)
    d_mlp_input = head_scatter(dot(d_gate_mlp, mlp_gate, 0, 1) + dot(d_up_mlp, mlp_up, 0, 1))
    scaled_mid = d_mlp_input * norm2_gain
    norm2_part = jnp.sum(d_mlp_input * unit_mid, axis=0)
    d_middle = out_cotangent.astype(F32) + scale_mid * (
        scaled_mid - unit_mid * jnp.mean(scaled_mid * unit_mid, axis=-1, keepdims=True)
    )
    d_attn = d_middle.astype(BF)
    if wide:
        sent, kept1 = slices(1)
        d_attn, got2, sent, kept1 = together(d_attn, got2, sent, kept1)
        got1 = shift(sent, 0, 1)
        far = plus(kept2, got2)
        h = far.shape[0] // 32 * 16
        a_far, b_far = shift(far[:h], 1, 0), shift(far[h:], 3, 0)
    d_attn_group = head_gather(d_attn)
    d_gated = dot(d_attn_group, out_weight, 1, 1)
    out_weight_grad = dot(gated_out, d_attn_group, 0, 0).astype(BF)
    d_post = d_gated * gate_act
    d_gate_pre = gelu_back(d_gated * post_out)[0].astype(BF)
    post_gain_part = jnp.sum(d_post * z_hat, axis=0)
    post_bias_part = jnp.sum(d_post, axis=0)
    d_zhat = d_post * post_gain
    back_sums = lax.psum((jnp.sum(d_zhat, axis=-1), jnp.sum(d_zhat * z_hat, axis=-1)), "head")
    d_z = inv_scale * (
        d_zhat - back_sums[0][:, None] / model_width - z_hat * (back_sums[1][:, None] / model_width)
    )
    if wide:
        d_z, a_far, b_far = together(d_z, a_far, b_far)
    step_grads, seg_grad = K["sgrad"](d_z, q_eff, step_maps)
    if wide:
        seg_grad, got1, normed_all = together(seg_grad, got1, normed_all)
        ahead = plus(kept1, got1)
        up = jnp.concatenate([plus(ahead[:h], a_far), ahead[h:]], axis=0)
    if wide:
        all_grads, (sent3, kept3), (sent0, kept0) = seq_gather(seg_grad, slices(3), slices(0))
    else:
        all_grads, _ = seq_gather(seg_grad)
    if wide:
        out_slice = lax.psum_scatter(out_weight_grad, "seq", scatter_dimension=0, tiled=True)
        got3, got0 = shift(sent3, 0, 1), shift(sent0, 0, 1)
        all_grads, up = together(all_grads, up)
        from_left = shift(up, 1, 0)
    d_query, b_part, lam_part = K["qgrad"](query_rows, key_rows, rate_rows, d_z, errors, states, pt)
    d_key, d_value, d_rate, init_grad, packed = K["kgrad"](
        place, all_maps, all_maps, all_grads, key_rows, rate_rows, errors, states, vv,
        b_part, lam_part, step_maps, step_grads, d_query, d_gate_pre,
    )
    if wide:
        d_rate, packed, got3, from_left, out_slice = together(
            d_rate, packed, got3, from_left, out_slice
        )
        behind = plus(kept3, got3)
        down = jnp.concatenate([behind[:h], plus(behind[h:], b_far)], axis=0)
        first = shift(down, 3, 0).astype(F32) + from_left.astype(F32)
        first = (first + kept0.astype(F32) + got0.astype(F32)).astype(BF)
    d_rate_pre = (d_rate * rate_scale * rate_sig * (1.0 - rate_sig)).astype(BF)
    scale_part = jnp.sum(d_rate * rate_sig, axis=0)
    total = dot(d_query, query_weight, 1, 1)
    total = total + dot(d_key, key_weight, 1, 1)
    total = total + dot(d_value, value_weight, 1, 1)
    total = total + dot(d_gate_pre, gate_weight, 1, 1)
    d_normed = head_scatter(total + dot(d_rate_pre, rate_weight, 1, 1))
    scaled_in = d_normed * norm1_gain
    norm1_part = jnp.sum(d_normed * unit_in, axis=0)
    input_grad = d_middle + scale_in * (
        scaled_in - unit_in * jnp.mean(scaled_in * unit_in, axis=-1, keepdims=True)
    )
    block_out = (middle + head_scatter(dot(hidden, mlp_down, 0, 0))).astype(BF)

    if wide:
        packed = lax.all_to_all(packed, "seq", split_axis=0, concat_axis=0, tiled=True)
        packed = packed.reshape(segs * tokens, packed.shape[2])
        left, crossed = gather1(first)
        left, crossed, packed, first = together(left, crossed, packed, first)
        own = dot(packed, normed_all, 0, 0).astype(BF)
        right, crossed_left = gather2(first, left)
        left, right, crossed_left = together(left, right, crossed_left)
        far_a, far_b, crossed_right = gather3(first, left, right)
        norm_parts = lax.psum((norm1_part, norm2_part), "head")
        ends = [0]
        extra = [d_rate_pre.reshape(-1)]
        for v in (scale_part, post_gain_part, post_bias_part, *norm_parts):
            extra.append(halves(v).reshape(-1))
        for v in extra:
            ends.append(ends[-1] + v.shape[0])
        extra = jnp.concatenate(extra + [jnp.zeros((16 * model_width - ends[-1],), BF)])
        second = jnp.concatenate([own, out_slice, extra.reshape(16, model_width)], axis=0)
        far_a, far_b, crossed_right, second = together(far_a, far_b, crossed_right, second)
        far, crossed_far = gather4(far_a, far_b)
        left2, crossed2 = gather1(second)
        far, crossed_far, left2, crossed2, second = together(
            far, crossed_far, left2, crossed2, second
        )
        right2, crossed_left2 = gather2(second, left2)
        pieces = (first, right, far, left, crossed, crossed_right, crossed_far, crossed_left)
        plan = tuple((t * rows, rows, False) for t in range(3))
        mlp_sums = finish(pieces, plan, (width,) * 3, "mlp_finish")
        left2, right2, crossed_left2 = together(left2, right2, crossed_left2)
        far_a, far_b, crossed_right2 = gather3(second, left2, right2)
        far_a, far_b, crossed_right2, mlp_sums = together(far_a, far_b, crossed_right2, mlp_sums)
        gate_sum, up_sum, down_sum = mlp_sums
        far2, crossed_far2 = gather4(far_a, far_b)
        full = segs * HW
        pieces = (
            second, right2, far2, left2, crossed2, crossed_right2, crossed_far2, crossed_left2
        )
        plan = tuple((t * HW, HW, t < 4) for t in range(5))
        query_sum, key_sum, value_sum, pre_sum, out_sum = finish(
            pieces, plan, (full,) * 5, "head_finish"
        )
        gate_sum, up_sum = gate_sum.T, up_sum.T
        shared = jnp.stack([v[-16:] for v in pieces]).reshape(segs, -1)
        shared = shared[jnp.argsort(slots())]
        from_all = [shared[:, s:e] for s, e in zip(ends[:-1], ends[1:])]
        d_rate_all = from_all[0].reshape(segs * tokens, local_heads)
        totals = [jnp.sum(v.astype(F32).reshape(2 * segs, -1), axis=0) for v in from_all[1:]]
        small = (
            dot(normed_all, d_rate_all, 0, 0),
            jnp.sum(d_rate_all.astype(F32), axis=0),
            *totals[:3],
        )
        gain_grads = totals[3:]
    else:
        grads = (
            dot(hidden, group_cot),
            dot(mlp_group, d_gate_mlp, 0, 1),
            dot(mlp_group, d_up_mlp, 0, 1),
            dot(group_in, d_query, 0, 0),
            dot(group_in, d_key, 0, 0),
            dot(group_in, d_value, 0, 0),
            dot(group_in, d_gate_pre, 0, 0),
            out_weight_grad,
        )
        sums = lax.psum(tuple(g.astype(BF) for g in grads), "seq")
        down_sum, gate_sum, up_sum, query_sum, key_sum, value_sum, pre_sum, out_sum = (
            s.astype(F32) for s in sums
        )
        small = lax.psum(
            (
                dot(group_in, d_rate_pre, 0, 0),
                jnp.sum(d_rate_pre.astype(F32), axis=0),
                scale_part,
                post_gain_part,
                post_bias_part,
            ),
            "seq",
        )
        gain_grads = lax.psum((norm1_part, norm2_part), everywhere)
    return (
        block_out,
        input_grad,
        gain_grads[0],
        query_sum,
        key_sum,
        value_sum,
        pre_sum,
        small[0],
        small[1],
        small[2],
        init_grad[:, :HW, :HW],
        init_grad[:, HW, :HW],
        small[3],
        small[4],
        out_sum,
        gain_grads[1],
        gate_sum,
        up_sum,
        down_sum,
    )


def solution(mesh):
    in_specs = (
        P(("seq", "head"), None),
        P(),
        P(None, "head"),
        P(None, "head"),
        P(None, "head"),
        P(None, "head"),
        P(None, "head"),
        P("head"),
        P("head"),
        P("head", None, None),
        P("head", None),
        P("head"),
        P("head"),
        P("head", None),
        P(),
        P(None, "head"),
        P(None, "head"),
        P("head", None),
        P(("seq", "head"), None),
    )
    out_specs = (
        P(("seq", "head"), None),
        P(("seq", "head"), None),
        P(),
        P(None, "head"),
        P(None, "head"),
        P(None, "head"),
        P(None, "head"),
        P(None, "head"),
        P("head"),
        P("head"),
        P("head", None, None),
        P("head", None),
        P("head"),
        P("head"),
        P("head", None),
        P(),
        P(None, "head"),
        P(None, "head"),
        P("head", None),
    )
    return jax.shard_map(body, mesh=mesh, in_specs=in_specs, out_specs=out_specs, check_vma=False)
```

```python
import functools
import jax, jax.numpy as jnp
from jax import lax
from jax.experimental import pallas as pl
from jax.experimental.pallas import tpu as pltpu
from jax.sharding import PartitionSpec as P

CHUNK=128
MB=16
F32=jnp.float32; BF=jnp.bfloat16
LN=128
HW=64
VL=48*1024*1024

def mm(a,b,ca,cb):
    return lax.dot_general(a.astype(BF),b.astype(BF),(((ca,),(cb,)),((),())),preferred_element_type=F32)
def nn(a,b): return mm(a,b,1,0)
def nt(a,b): return mm(a,b,1,1)
def tn(a,b): return mm(a,b,0,0)
def split(a):
    hi=a.astype(BF)
    return hi,(a-hi.astype(F32)).astype(BF)
def nn3(a,b):
    ah,al=a; bh,bl=b
    return nn(ah,bh)+(nn(ah,bl)+nn(al,bh))

def lanes(shape): return lax.broadcasted_iota(jnp.int32,shape,1)
def rows(shape): return lax.broadcasted_iota(jnp.int32,shape,0)
def head_of(x,odd):
    y=pltpu.roll(x,HW,1) if odd else x
    return jnp.where(lanes(x.shape)<HW,y,0.0)
def aug(x): return jnp.where(lanes(x.shape)==HW,1.0,x)
def pair(a,b):
    return jnp.where(lanes(a.shape)<HW,a,pltpu.roll(b,HW,1))
def column(block,h):
    return jnp.sum(jnp.where(lanes(block.shape)==h,block,0.0),axis=1,keepdims=True)
def causal(C): return rows((C,C))>=lanes((C,C))
def earlier(C): return (rows((C,C))>>4)>(lanes((C,C))>>4)
def level(C,b):
    i=rows((C,C)); j=lanes((C,C))
    return ((i>>(b+1))==(j>>(b+1)))&((i>>b)>(j>>b))

def block_inverses(lows,C):
    b=4
    mask=level(C,b)
    ys=[jnp.where(mask,-low,0.0) for low in lows]
    b+=1
    while (1<<b)<C:
        mask=level(C,b)
        parts=[jnp.where(mask,low,0.0) for low in lows]
        yb=[y.astype(BF) for y in ys]
        zs=[p+nn(y,p) for y,p in zip(yb,parts)]
        ys=[y-(z+nn(z,b2)) for y,z,b2 in zip(ys,zs,yb)]
        b+=1
    return ys

def map_kernel(C,k_ref,v_ref,r_ref,t_ref,uw_ref,x_ref,y_ref):
    p=pl.program_id(0)
    N=k_ref.shape[0]
    last=y_ref.shape[0]-1
    @pl.when(p==0)
    def _(): y_ref[last]=jnp.zeros((80,LN),BF)
    units=[(odd,c,pl.ds(c*C,C)) for c in range(N//C) for odd in range(2)]
    mask=earlier(C)
    eye=jnp.where(rows((C,C))==lanes((C,C)),1.0,0.0)
    ks=[head_of(k_ref[sl,:],odd) for odd,c,sl in units]
    kws=[jnp.concatenate([aug(k),head_of(v_ref[sl,:],odd)-k],axis=1) for k,(odd,c,sl) in zip(ks,units)]
    krs=[(kw[:,:LN]*column(r_ref[sl,:],2*p+odd)).astype(BF) for kw,(odd,c,sl) in zip(kws,units)]
    lows=[jnp.where(mask,nt(kw[:,:LN],kr),0.0) for kw,kr in zip(kws,krs)]
    ys=block_inverses(lows,C)
    total=[None,None]
    uws=[kw+nn(y,kw) for y,kw in zip(ys,kws)]
    xcs=[tn(kr,jnp.where(lanes(uw.shape)<LN,-uw,uw)) for kr,uw in zip(krs,uws)]
    for (odd,c,sl),y,uw,xc in zip(units,ys,uws,xcs):
        t_ref[odd,c]=(y+eye).astype(BF)
        uw_ref[odd,sl,:]=uw.astype(BF)
        x_ref[odd,c]=xc.astype(BF)
        total[odd]=xc if total[odd] is None else total[odd]+xc+nn(xc[:,:LN],total[odd])
    for odd in range(2):
        h=2*p+odd
        a=total[odd][:,:LN]; o=total[odd][:,LN:]
        y_ref[h]=pair(a,o)[:80].astype(BF)
        col=jnp.sum(jnp.where(lanes(a.shape)==HW,a,0.0),axis=1,keepdims=True)[:80]
        y_ref[last]=jnp.where(lanes((80,LN))==h,col,y_ref[last].astype(F32)).astype(BF)

def local_kernel(C,q_ref,k_ref,r_ref,t_ref,uw_ref,qe_ref,zo_ref,pt_ref,vv_ref):
    p=pl.program_id(0)
    N=q_ref.shape[0]
    mask=causal(C)
    for c in range(N//C):
        sl=pl.ds(c*C,C)
        offs=[]
        for odd in range(2):
            h=2*p+odd
            q=head_of(q_ref[sl,:],odd); qa=aug(q)
            ka=aug(head_of(k_ref[sl,:],odd))
            kr=ka*column(r_ref[sl,:],h)
            pm=jnp.where(mask,nt(qa,kr),0.0)
            t=t_ref[odd,c]
            puw=nn(pm,uw_ref[odd,sl,:])
            qe_ref[odd,sl,:]=(qa-puw[:,:LN]).astype(BF)
            offs.append(q+puw[:,LN:])
            pt_ref[odd,c]=nn(pm,t).astype(BF)
            vv_ref[odd,sl,:]=tn(t,kr).astype(BF)
        zo_ref[sl,:]=pair(offs[0],offs[1])

def unpack(y,yb,h):
    y=y.astype(F32)
    col=column(yb.astype(F32),h)
    ln=lanes(y.shape)
    a=jnp.where(ln<HW,y,jnp.where(ln==HW,col,0.0))
    o=jnp.where(ln<HW,pltpu.roll(y,HW,1),0.0)
    pad=jnp.zeros((LN-80,LN),F32)
    return jnp.concatenate([a,pad],0),jnp.concatenate([o,pad],0)

def start_of(is_ref,ib_ref,odd):
    s=jnp.concatenate([is_ref[odd],ib_ref[odd],jnp.zeros((LN-HW-1,HW),F32)],axis=0)
    return jnp.concatenate([s,jnp.zeros_like(s)],axis=1)

def forward_kernel(C,seg_ref,y_ref,yb_ref,is_ref,ib_ref,x_ref,uw_ref,qe_ref,zo_ref,z_ref,e_ref,s_ref):
    p=pl.program_id(0)
    N=zo_ref.shape[0]
    segs=y_ref.shape[0]
    seg=seg_ref[0]
    nc=N//C
    ss=[start_of(is_ref,ib_ref,odd) for odd in range(2)]
    for j in range(segs-1):
        at=seg_ref[1+j]
        on=jnp.where(j<seg,1.0,0.0)
        for odd in range(2):
            a,o=unpack(y_ref[at,odd],yb_ref[at,0],2*p+odd)
            ss[odd]=ss[odd]+on*(nn(a,ss[odd])+o)
    sbs=[[],[]]
    for c in range(nc):
        for odd in range(2):
            sb=ss[odd].astype(BF)
            sbs[odd].append(sb)
            x=x_ref[odd,c]
            ss[odd]=ss[odd]+nn(x[:,:LN],sb)+x[:,LN:].astype(F32)
    for c in range(nc):
        sl=pl.ds(c*C,C)
        add=[]
        for odd in range(2):
            sb=sbs[odd][c]
            s_ref[odd,c]=sb
            uw=uw_ref[odd,sl,:]
            e_ref[odd,sl,:]=(nn(uw[:,:LN],sb)-uw[:,LN:].astype(F32)).astype(BF)
            add.append(nn(qe_ref[odd,sl,:],sb))
        z_ref[sl,:]=zo_ref[sl,:]+pair(add[0],add[1])

def state_grad_kernel(C,dz_ref,qe_ref,x_ref,d_ref,dseg_ref):
    N=dz_ref.shape[0]
    outs=[]
    for odd in range(2):
        g=jnp.zeros((LN,LN),F32)
        for c in reversed(range(N//C)):
            sl=pl.ds(c*C,C)
            dz=head_of(dz_ref[sl,:],odd)
            d=tn(qe_ref[odd,sl,:],dz)
            d_ref[odd,c]=d
            g=g+tn(x_ref[odd,c][:,:LN],g)+d
        outs.append(g)
    dseg_ref[0]=pair(outs[0],outs[1])[:80].astype(BF)

def query_grad_kernel(C,q_ref,k_ref,r_ref,dz_ref,e_ref,s_ref,pt_ref,dq_ref,b_ref,l_ref):
    p=pl.program_id(0)
    N=q_ref.shape[0]
    mask=causal(C)
    for c in range(N//C):
        sl=pl.ds(c*C,C)
        outs=[]
        for odd in range(2):
            h=2*p+odd
            dz=head_of(dz_ref[sl,:],odd); dzb=dz.astype(BF)
            qa=aug(head_of(q_ref[sl,:],odd))
            ka=aug(head_of(k_ref[sl,:],odd))
            kr=ka*column(r_ref[sl,:],h)
            fu=jnp.where(mask,-nt(dzb,e_ref[odd,sl,:]),0.0).astype(BF)
            outs.append(dz+nt(dzb,s_ref[odd,c])+nn(fu,kr))
            b_ref[odd,sl,:]=tn(fu,qa).astype(BF)
            l_ref[odd,sl,:]=-tn(pt_ref[odd,c],dzb)
        dq_ref[sl,:]=pair(outs[0],outs[1]).astype(BF)

def key_grad_kernel(C,seg_ref,y_ref,yb_ref,da_ref,k_ref,r_ref,e_ref,s_ref,vv_ref,b_ref,l_ref,x_ref,d_ref,dq_ref,dg_ref,dk_ref,dv_ref,dr_ref,gi_ref,pk_ref):
    p=pl.program_id(0)
    N=k_ref.shape[0]
    segs=y_ref.shape[0]
    seg=seg_ref[0]
    @pl.when(p==0)
    def _(): dr_ref[...]=jnp.zeros_like(dr_ref)
    pad=jnp.zeros((LN-80,LN),F32)
    nc=N//C
    full=[jnp.zeros((LN,LN),F32) for _ in range(2)]
    gs=[jnp.zeros((LN,LN),F32) for _ in range(2)]
    for j in reversed(range(segs)):
        at=seg_ref[1+j]
        for odd in range(2):
            a,_=unpack(y_ref[at,odd],yb_ref[at,0],2*p+odd)
            d=jnp.concatenate([head_of(da_ref[at,0].astype(F32),odd),pad],0)
            full[odd]=full[odd]+tn(a,full[odd])+d
            gs[odd]=jnp.where(j==seg+1,full[odd],gs[odd])
    for odd in range(2): gi_ref[odd]=full[odd][:72]
    gbs=[[None]*nc for _ in range(2)]
    for c in reversed(range(nc)):
        for odd in range(2):
            gb=gs[odd].astype(BF)
            gbs[odd][c]=gb
            gs[odd]=gs[odd]+tn(x_ref[odd,c][:,:LN],gb)+d_ref[odd,c]
    mask=earlier(C)
    for c in range(nc):
        sl=pl.ds(c*C,C)
        dks=[]; lams=[]
        for odd in range(2):
            h=2*p+odd
            gb=gbs[odd][c]
            ka=aug(head_of(k_ref[sl,:],odd))
            r=column(r_ref[sl,:],h)
            kr=ka*r
            e=e_ref[odd,sl,:]
            lam=l_ref[odd,sl,:]-nn(vv_ref[odd,sl,:],gb)
            lb=lam.astype(BF)
            hu=jnp.where(mask,-nt(lb,e),0.0).astype(BF)
            b=b_ref[odd,sl,:].astype(F32)+tn(hu,ka)-nt(e,gb)
            dks.append(r*b+nt(lb,s_ref[odd,c])+nn(hu,kr)+lam)
            lams.append(lam)
            dr=jnp.sum(ka*b,axis=1,keepdims=True)
            dr_ref[sl,:]=jnp.where(lanes((C,dr_ref.shape[1]))==h,dr,dr_ref[sl,:])
        dk_ref[sl,:]=pair(dks[0],dks[1]).astype(BF)
        dv_ref[sl,:]=-pair(lams[0],lams[1]).astype(BF)
        dq=dq_ref[sl,:].astype(F32); dg=dg_ref[sl,:].astype(F32)
        for odd in range(2):
            first=pair(head_of(dq,odd),dks[odd]); second=pair(-lams[odd],head_of(dg,odd))
            pk_ref[odd,sl,:]=jnp.concatenate([first,second],axis=1).astype(BF)

def params(): return pltpu.CompilerParams(dimension_semantics=("arbitrary",),vmem_limit_bytes=VL)
def S(shape,dt): return jax.ShapeDtypeStruct(shape,dt)

def specs(N,hl,C):
    nc=N//C
    d={}
    d["row"]=pl.BlockSpec((N,LN),lambda p,*_:(0,p))
    d["rate"]=pl.BlockSpec((N,hl),lambda p,*_:(0,0))
    d["cc"]=pl.BlockSpec((2,nc,C,C),lambda p,*_:(p,0,0,0))
    d["n256"]=pl.BlockSpec((2,N,2*LN),lambda p,*_:(p,0,0))
    d["n128"]=pl.BlockSpec((2,N,LN),lambda p,*_:(p,0,0))
    d["x"]=pl.BlockSpec((2,nc,LN,2*LN),lambda p,*_:(p,0,0,0))
    d["s"]=pl.BlockSpec((2,nc,LN,LN),lambda p,*_:(p,0,0,0))
    d["y"]=pl.BlockSpec((hl+1,80,LN),lambda p,*_:(0,0,0))
    return d

def build(N,hl,segs,C=128):
    nc=N//C; sp=specs(N,hl,C); G=(hl//2,)
    w=hl*HW
    K={}
    K["map"]=pl.pallas_call(functools.partial(map_kernel,C),grid=G,in_specs=[sp["row"],sp["row"],sp["rate"]],
        out_specs=[sp["cc"],sp["n256"],sp["x"],sp["y"]],
        out_shape=[S((hl,nc,C,C),BF),S((hl,N,2*LN),BF),S((hl,nc,LN,2*LN),BF),S((hl+1,80,LN),BF)],compiler_params=params(),name="segment_maps")
    K["local"]=pl.pallas_call(functools.partial(local_kernel,C),grid=G,in_specs=[sp["row"],sp["row"],sp["rate"],sp["cc"],sp["n256"]],
        out_specs=[sp["n128"],sp["row"],sp["cc"],sp["n128"]],
        out_shape=[S((hl,N,LN),BF),S((N,w),F32),S((hl,nc,C,C),BF),S((hl,N,LN),BF)],compiler_params=params(),name="local_parts")
    yall=pl.BlockSpec((segs,2,80,LN),lambda p,*_:(0,p,0,0)); yball=pl.BlockSpec((segs,1,80,LN),lambda p,*_:(0,hl,0,0))
    dall=pl.BlockSpec((segs,1,80,LN),lambda p,*_:(0,p,0,0))
    ist=pl.BlockSpec((2,HW,HW),lambda p,*_:(p,0,0)); ibs=pl.BlockSpec((2,1,HW),lambda p,*_:(p,0,0))
    def gs(i,o): return pltpu.PrefetchScalarGridSpec(num_scalar_prefetch=1,grid=G,in_specs=i,out_specs=o)
    K["forward"]=pl.pallas_call(functools.partial(forward_kernel,C),grid_spec=gs([yall,yball,ist,ibs,sp["x"],sp["n256"],sp["n128"],sp["row"]],[sp["row"],sp["n128"],sp["s"]]),
        out_shape=[S((N,w),F32),S((hl,N,LN),BF),S((hl,nc,LN,LN),BF)],compiler_params=params(),name="forward_states")
    K["sgrad"]=pl.pallas_call(functools.partial(state_grad_kernel,C),grid=G,in_specs=[sp["row"],sp["n128"],sp["x"]],
        out_specs=[sp["s"],pl.BlockSpec((1,80,LN),lambda p:(p,0,0))],out_shape=[S((hl,nc,LN,LN),F32),S((hl//2,80,LN),BF)],compiler_params=params(),name="state_grads")
    K["qgrad"]=pl.pallas_call(functools.partial(query_grad_kernel,C),grid=G,in_specs=[sp["row"],sp["row"],sp["rate"],sp["row"],sp["n128"],sp["s"],sp["cc"]],
        out_specs=[sp["row"],sp["n128"],sp["n128"]],out_shape=[S((N,w),BF),S((hl,N,LN),BF),S((hl,N,LN),F32)],compiler_params=params(),name="query_grads")
    K["kgrad"]=pl.pallas_call(functools.partial(key_grad_kernel,C),grid_spec=gs([yall,yball,dall,sp["row"],sp["rate"],sp["n128"],sp["s"],sp["n128"],sp["n128"],sp["n128"],sp["x"],sp["s"],sp["row"],sp["row"]],
        [sp["row"],sp["row"],sp["rate"],pl.BlockSpec((2,72,LN),lambda p,*_:(p,0,0)),sp["n256"]]),
        out_shape=[S((N,w),BF),S((N,w),BF),S((N,hl),F32),S((hl,72,LN),F32),S((hl,N,2*LN),BF)],compiler_params=params(),name="key_grads")
    return K


EPSILON = 1e-06


def grid_of():
    seq = lax.axis_size("seq")
    x = max(lax.axis_size("head") // 2, 1)
    if seq % x:
        x = 1
    return seq // x, x


def shift(v, dz, dx):
    Z, X = grid_of()
    pairs = [(z * X + x, ((z + dz) % Z) * X + (x + dx) % X) for z in range(Z) for x in range(X)]
    return lax.ppermute(v, "seq", pairs)


def seq_gather(v, between, *later):
    Z, X = grid_of()
    i = lax.axis_index("seq")
    j = jnp.arange(Z * X, dtype=jnp.int32)
    if (Z, X) != (4, 2):
        return (lax.all_gather(v, "seq", axis=0, tiled=False), j), between
    other = shift(v, 0, 1)
    if later:
        other, later = together(other, later)
    both = jnp.stack([v, other])
    left = shift(both, 1, 0)
    right = shift(both, 3, 0)
    left, right, between = together(left, right, between)
    far0 = shift(left[:1], 1, 0)
    far1 = shift(right[1:], 3, 0)
    z, x = i // X, i % X
    every = jnp.concatenate([both, right, far0, far1, left])
    order = ((j // X - z) % Z) * X + (j % X - x) % X
    return (every, order, *later), between


def head_shift(v, dy, dc):
    H = lax.axis_size("head")
    Y = H // 2
    pairs = [(y * 2 + c, ((y + dy) % Y) * 2 + (c + dc) % 2) for y in range(Y) for c in range(2)]
    return lax.ppermute(v, "head", pairs)


def head_gather(v, across=None):
    H = lax.axis_size("head")
    if H != 4:
        return lax.all_gather(v, "head", axis=0, tiled=True)
    i = lax.axis_index("head")
    y, c = i // 2, i % 2
    mine = jnp.stack([v, head_shift(v, 1, 0) if across is None else across])
    other = head_shift(mine, 0, 1)
    a = jnp.where(c == 0, mine, other)
    b = jnp.where(c == 0, other, mine)
    rows = [jnp.where(y == 0, a[0], a[1]), jnp.where(y == 0, b[0], b[1])]
    rows += [jnp.where(y == 0, a[1], a[0]), jnp.where(y == 0, b[1], b[0])]
    return jnp.concatenate(rows, axis=0)


def head_scatter(v, hold=None):
    H = lax.axis_size("head")
    v = v.astype(BF)
    if H != 4:
        return lax.psum_scatter(v, "head", scatter_dimension=0, tiled=True).astype(F32)
    i = lax.axis_index("head")
    y, c = i // 2, i % 2
    v = v.reshape(2, 2, v.shape[0] // 4, v.shape[1])
    got = head_shift(jnp.where(c == 0, v[:, 1], v[:, 0]), 0, 1)
    half = (jnp.where(c == 0, v[:, 0], v[:, 1]).astype(F32) + got.astype(F32)).astype(BF)
    back = head_shift(jnp.where(y == 0, half[1], half[0]), 1, 0)
    if hold is not None:
        back, hold = together(back, hold)
    total = jnp.where(y == 0, half[0], half[1]).astype(F32) + back.astype(F32)
    return total if hold is None else (total, hold)


def gelu_tanh(values):
    return jax.nn.gelu(values, approximate=True)


def dot(a, b, ca=1, cb=0):
    return lax.dot_general(a, b, (((ca,), (cb,)), ((), ())), preferred_element_type=F32)


def together(*values):
    return lax.optimization_barrier(values)


def at(v, i, axis=0):
    return lax.dynamic_index_in_dim(v, i, axis, keepdims=False)


def plus(a, b):
    return (a.astype(F32) + b.astype(F32)).astype(BF)


def slices_kernel(at_ref, g0, u0, h0, g1, u1, h1, x_ref, c_ref, send_ref, keep_ref):
    rows = g0.shape[0]
    for g, u, h, out in ((g0, u0, h0, send_ref), (g1, u1, h1, keep_ref)):
        for t, (left, right) in enumerate(((g, x_ref), (u, x_ref), (h, c_ref))):
            out[pl.ds(t * rows, rows), :] = dot(left[...], right[...]).astype(BF)


def mlp_slices(k, rows, d_gate, d_up, hidden, mlp_group, cot_group):
    i = lax.axis_index("seq")
    z, x = i // 2, i % 2
    to = ((z + k) % 4) * 2
    which = jnp.stack([to + 1 - x, to + x]).astype(jnp.int32)
    N, D = mlp_group.shape
    tile = min(D, 512)
    act = [pl.BlockSpec((rows, N), lambda j, o, n=n: (o[n], 0)) for n in (0, 1)]
    col = pl.BlockSpec((N, tile), lambda j, o: (0, j))
    out = pl.BlockSpec((3 * rows, tile), lambda j, o: (0, j))
    return pl.pallas_call(
        slices_kernel,
        grid_spec=pltpu.PrefetchScalarGridSpec(
            num_scalar_prefetch=1,
            grid=(D // tile,),
            in_specs=[act[0]] * 3 + [act[1]] * 3 + [col, col],
            out_specs=[out, out],
        ),
        out_shape=[jax.ShapeDtypeStruct((3 * rows, D), BF)] * 2,
        compiler_params=params(),
        name="mlp_slices",
    )(which, d_gate, d_up, hidden, d_gate, d_up, hidden, mlp_group, cot_group)


def slots():
    i = lax.axis_index("seq")
    z, x = i // 2, i % 2
    zs = (z + jnp.arange(4, dtype=jnp.int32)) % 4
    return jnp.concatenate([zs * 2 + x, zs * 2 + 1 - x]).astype(jnp.int32)


def finish_kernel(plan, at_ref, *refs):
    pieces, outs, scratch = refs[:8], refs[8:-1], refs[-1]
    for out, (first, rows, turned) in zip(outs, plan):
        for slot, ref in enumerate(pieces):
            start = pl.multiple_of(at_ref[slot] * rows, 16)
            scratch[pl.ds(start, rows), :] = ref[pl.ds(first, rows), :].astype(F32)
        if turned:
            out[...] = scratch[pl.ds(0, out.shape[1]), :].T
        else:
            out[...] = scratch[pl.ds(0, out.shape[0]), :]


def finish(pieces, plan, widths, name):
    R, D = pieces[0].shape
    out_specs, out_shape = [], []
    for w, (_, _, turned) in zip(widths, plan):
        if turned:
            out_specs.append(pl.BlockSpec((LN, w), lambda i, o: (i, 0)))
            out_shape.append(jax.ShapeDtypeStruct((D, w), F32))
        else:
            out_specs.append(pl.BlockSpec((w, LN), lambda i, o: (0, i)))
            out_shape.append(jax.ShapeDtypeStruct((w, D), F32))
    return pl.pallas_call(
        functools.partial(finish_kernel, plan),
        grid_spec=pltpu.PrefetchScalarGridSpec(
            num_scalar_prefetch=1,
            grid=(D // LN,),
            in_specs=[pl.BlockSpec((R, LN), lambda i, o: (0, i))] * 8,
            out_specs=out_specs,
            scratch_shapes=[pltpu.VMEM((8 * max(p[1] for p in plan), LN), F32)],
        ),
        out_shape=out_shape,
        compiler_params=params(),
        name=name,
    )(slots(), *pieces)


def put_heads_kernel(at_ref, own_ref, other_ref, *refs):
    outs = refs[-5:]
    for t, out in enumerate(outs):
        own = own_ref[pl.ds(t * HW, HW), :].astype(F32)
        other = other_ref[pl.ds(t * HW, HW), :].astype(F32)
        even = at_ref[1] == 0
        both = jnp.concatenate([jnp.where(even, own, other), jnp.where(even, other, own)], axis=0)
        out[...] = both.T if t < 4 else both


def put_heads(k, own, other, before):
    i = lax.axis_index("seq")
    place = jnp.stack([(i // 2 + k) % 4, i % 2]).astype(jnp.int32)
    R, D = own.shape
    width = 8 * HW
    tile = min(D, 512)
    piece = pl.BlockSpec((R, tile), lambda j, o: (0, j))
    turned = pl.BlockSpec((tile, LN), lambda j, o: (j, o[0]))
    straight = pl.BlockSpec((LN, tile), lambda j, o: (o[0], j))
    before = [] if before is None else list(before)
    return pl.pallas_call(
        put_heads_kernel,
        grid_spec=pltpu.PrefetchScalarGridSpec(
            num_scalar_prefetch=1,
            grid=(D // tile,),
            in_specs=[piece, piece] + [pl.BlockSpec(memory_space=pl.ANY)] * len(before),
            out_specs=[turned] * 4 + [straight],
        ),
        out_shape=[jax.ShapeDtypeStruct((D, width), F32)] * 4
        + [jax.ShapeDtypeStruct((width, D), F32)],
        input_output_aliases={3 + n: n for n in range(len(before))},
        compiler_params=params(),
        name="put_heads",
    )(place, own, other, *before)


def rows_of(values, D):
    values = jnp.concatenate(values)
    return jnp.concatenate([values, jnp.zeros((16 * D - values.shape[0],), BF)]).reshape(16, D)


def in_order(pieces):
    i = lax.axis_index("seq")
    z, x = i // 2, i % 2
    j = jnp.arange(8, dtype=jnp.int32)
    slot = (j // 2 - z) % 4 + 4 * ((j % 2 - x) % 2)
    return jnp.stack(pieces)[slot].reshape(8, -1)


def halves(v):
    hi = v.astype(BF)
    return jnp.stack([hi, (v - hi.astype(F32)).astype(BF)])


def body(
    block_input,
    norm1_gain,
    query_weight,
    key_weight,
    value_weight,
    gate_weight,
    rate_weight,
    rate_bias,
    rate_scale,
    init_state,
    init_bias,
    post_gain,
    post_bias,
    out_weight,
    norm2_gain,
    mlp_gate,
    mlp_up,
    mlp_down,
    out_cotangent,
):
    local_heads = init_state.shape[0]
    model_width = block_input.shape[1]
    width = mlp_gate.shape[1]
    segs = lax.axis_size("seq")
    heads = lax.axis_size("head")
    tokens = block_input.shape[0] * heads
    K = build(tokens, local_heads, segs, CHUNK)
    seg = lax.axis_index("seq").astype(jnp.int32).reshape(1)
    wide = local_heads == segs and tokens * segs * model_width <= 1 << 23 and grid_of() == (4, 2)
    everywhere = ("seq", "head")

    input_f32 = block_input.astype(F32)
    scale_in = lax.rsqrt(jnp.mean(input_f32 * input_f32, axis=-1, keepdims=True) + EPSILON)
    unit_in = input_f32 * scale_in
    normed = (unit_in * norm1_gain).astype(BF)
    group_in = head_gather(normed)
    key_rows = dot(group_in, key_weight)
    value_rows = dot(group_in, value_weight)
    rate_pre = dot(group_in, rate_weight) + rate_bias
    rate_sig = jax.nn.sigmoid(rate_pre)
    rate_rows = rate_sig * rate_scale
    inv, uw, step_maps, seg_map = K["map"](key_rows, value_rows, rate_rows)
    cot_late, seg_map = together(out_cotangent, seg_map)
    cot_across = head_shift(cot_late, 1, 0) if heads == 4 else cot_late
    query_rows = dot(group_in, query_weight)
    local = K["local"](query_rows, key_rows, rate_rows, inv, uw)
    (all_maps, order), (local, cot_across) = seq_gather(seg_map, (local, cot_across))
    group_cot = head_gather(out_cotangent, cot_across)
    q_eff, z_off, pt, vv = local
    place = jnp.concatenate([seg, order])
    if wide:
        normed_late, all_maps = together(normed, all_maps)
        normed_all = lax.all_gather(normed_late, everywhere, axis=0, tiled=True)
    gate_pre = dot(group_in, gate_weight)
    z_rows, errors, states = K["forward"](
        place, all_maps, all_maps, init_state, init_bias[:, None, :], step_maps, uw, q_eff, z_off
    )
    stat_sums = lax.psum((jnp.sum(z_rows, axis=-1), jnp.sum(z_rows * z_rows, axis=-1)), "head")
    row_mean = stat_sums[0] / model_width
    row_var = stat_sums[1] / model_width - row_mean * row_mean
    inv_scale = lax.rsqrt(row_var + EPSILON)[:, None]
    z_hat = (z_rows - row_mean[:, None]) * inv_scale
    post_out = z_hat * post_gain + post_bias
    gate_act, gelu_back = jax.vjp(gelu_tanh, gate_pre)
    gated_out = (gate_act * post_out).astype(BF)
    middle = input_f32 + head_scatter(dot(gated_out, out_weight))
    scale_mid = lax.rsqrt(jnp.mean(middle * middle, axis=-1, keepdims=True) + EPSILON)
    unit_mid = middle * scale_mid
    mlp_input = (unit_mid * norm2_gain).astype(BF)
    mlp_group = head_gather(mlp_input)
    gate_mlp = dot(mlp_gate, mlp_group, 0, 1)
    up_mlp = dot(mlp_up, mlp_group, 0, 1)
    silu_gate, silu_back = jax.vjp(jax.nn.silu, gate_mlp)
    hidden = (silu_gate * up_mlp).astype(BF)
    d_hidden = dot(mlp_down, group_cot, 1, 1)
    d_gate_mlp = silu_back(d_hidden * up_mlp)[0].astype(BF)
    d_up_mlp = (d_hidden * silu_gate).astype(BF)
    if wide:
        rows = -(-width // (16 * segs)) * 16
        slices = lambda k: mlp_slices(k, rows, d_gate_mlp, d_up_mlp, hidden, mlp_group, group_cot)
        d_gate_mlp, (sent, kept2) = together(d_gate_mlp, slices(2))
        got2 = shift(sent, 0, 1)
    d_mlp_part = dot(d_gate_mlp, mlp_gate, 0, 1) + dot(d_up_mlp, mlp_up, 0, 1)
    if wide:
        d_mlp_input, (got2, (sent1, kept1)) = head_scatter(d_mlp_part, (got2, slices(1)))
    else:
        d_mlp_input = head_scatter(d_mlp_part)
    scaled_mid = d_mlp_input * norm2_gain
    norm2_part = jnp.sum(d_mlp_input * unit_mid, axis=0)
    d_middle = out_cotangent.astype(F32) + scale_mid * (
        scaled_mid - unit_mid * jnp.mean(scaled_mid * unit_mid, axis=-1, keepdims=True)
    )
    d_attn = d_middle.astype(BF)
    if wide:
        got1 = shift(sent1, 0, 1)
        far = plus(kept2, got2)
        h = far.shape[0] // 32 * 16
        a_far, b_far = shift(far[:h], 1, 0), shift(far[h:], 3, 0)
        across = head_shift(d_attn, 1, 0)
        across, got1, a_far, b_far = together(across, got1, a_far, b_far)
        d_attn_group = head_gather(d_attn, across)
        ahead = plus(kept1, got1)
        up = jnp.concatenate([plus(ahead[:h], a_far), ahead[h:]], axis=0)
        up, (sent, kept3) = together(up, slices(3))
        from_left, got3 = shift(up, 1, 0), shift(sent, 0, 1)
    else:
        d_attn_group = head_gather(d_attn)
    d_gated = dot(d_attn_group, out_weight, 1, 1)
    out_weight_grad = dot(gated_out, d_attn_group, 0, 0).astype(BF)
    d_post = d_gated * gate_act
    d_gate_pre = gelu_back(d_gated * post_out)[0].astype(BF)
    post_gain_part = jnp.sum(d_post * z_hat, axis=0)
    post_bias_part = jnp.sum(d_post, axis=0)
    d_zhat = d_post * post_gain
    back_sums = lax.psum((jnp.sum(d_zhat, axis=-1), jnp.sum(d_zhat * z_hat, axis=-1)), "head")
    d_z = inv_scale * (
        d_zhat - back_sums[0][:, None] / model_width - z_hat * (back_sums[1][:, None] / model_width)
    )
    mlp_out = head_scatter(dot(hidden, mlp_down, 0, 0))
    d_z, mlp_out = together(d_z, mlp_out)
    step_grads, seg_grad = K["sgrad"](d_z, q_eff, step_maps)
    query_parts = K["qgrad"](query_rows, key_rows, rate_rows, d_z, errors, states, pt)
    if wide:
        (all_grads, _, (sent, kept0)), query_parts = seq_gather(seg_grad, query_parts, slices(0))
        got0 = shift(sent, 0, 1)
        all_grads, got3, from_left, normed_all = together(all_grads, got3, from_left, normed_all)
        behind = plus(kept3, got3)
        down = jnp.concatenate([behind[:h], plus(behind[h:], b_far)], axis=0)
        from_right = shift(down, 3, 0)
        out_slice = lax.psum_scatter(out_weight_grad, "seq", scatter_dimension=0, tiled=True)
    else:
        (all_grads, _), query_parts = seq_gather(seg_grad, query_parts)
    d_query, b_part, lam_part = query_parts
    d_key, d_value, d_rate, init_grad, packed = K["kgrad"](
        place, all_maps, all_maps, all_grads, key_rows, rate_rows, errors, states, vv,
        b_part, lam_part, step_maps, step_grads, d_query, d_gate_pre,
    )
    if wide:
        packed, out_slice = together(packed, out_slice)
        first = from_left.astype(F32) + from_right.astype(F32)
        first = (first + kept0.astype(F32) + got0.astype(F32)).astype(BF)
    d_rate_pre = (d_rate * rate_scale * rate_sig * (1.0 - rate_sig)).astype(BF)
    scale_part = jnp.sum(d_rate * rate_sig, axis=0)
    total = dot(d_query, query_weight, 1, 1)
    total = total + dot(d_key, key_weight, 1, 1)
    total = total + dot(d_value, value_weight, 1, 1)
    total = total + dot(d_gate_pre, gate_weight, 1, 1)
    d_normed = head_scatter(total + dot(d_rate_pre, rate_weight, 1, 1))
    scaled_in = d_normed * norm1_gain
    norm1_part = jnp.sum(d_normed * unit_in, axis=0)
    input_grad = d_middle + scale_in * (
        scaled_in - unit_in * jnp.mean(scaled_in * unit_in, axis=-1, keepdims=True)
    )
    block_out = (middle + mlp_out).astype(BF)

    if wide:
        extra = [d_rate_pre.reshape(-1)]
        for v in (scale_part, post_gain_part, post_bias_part):
            extra.append(halves(v).reshape(-1))
        first = jnp.concatenate([first, rows_of(extra, model_width)], axis=0)
        crossed = shift(first, 0, 1)
        packed = lax.all_to_all(packed, "seq", split_axis=0, concat_axis=0, tiled=True)
        packed, crossed, first = together(packed, crossed, first)
        left = shift(first, 1, 0)
        packed = packed.reshape(segs * tokens, packed.shape[2])
        own = dot(packed, normed_all, 0, 0).astype(BF)
        norm_parts = lax.psum((norm1_part, norm2_part), "head")
        norm_rows = rows_of([halves(v).reshape(-1) for v in norm_parts], model_width)
        second = jnp.concatenate([own, out_slice, norm_rows], axis=0)
        crossed2 = shift(second, 0, 1)
        left, crossed2, first, second = together(left, crossed2, first, second)
        right, crossed_left = shift(first, 3, 0), shift(left, 0, 1)
        left, right, crossed_left = together(left, right, crossed_left)
        h = first.shape[0] // 32 * 16
        far_a, far_b = shift(left[:h], 1, 0), shift(right[h:], 3, 0)
        crossed_right = shift(right, 0, 1)
        far_a, far_b, crossed_right, second = together(far_a, far_b, crossed_right, second)
        far = jnp.concatenate([far_a, far_b], axis=0)
        crossed_far, left2 = shift(far, 0, 1), shift(second, 1, 0)
        head_sums = put_heads(0, second, crossed2, None)
        crossed_far, left2, second, head_sums = together(crossed_far, left2, second, head_sums)
        right2, crossed_left2 = shift(second, 3, 0), shift(left2, 0, 1)
        pieces = (first, right, far, left, crossed, crossed_right, crossed_far, crossed_left)
        plan = tuple((t * rows, rows, False) for t in range(3))
        mlp_sums = finish(pieces, plan, (width,) * 3, "mlp_finish")
        left2, right2, crossed_left2, mlp_sums = together(left2, right2, crossed_left2, mlp_sums)
        h = second.shape[0] // 32 * 16
        far_a, far_b = shift(left2[:h], 1, 0), shift(right2[h:], 3, 0)
        crossed_right2 = shift(right2, 0, 1)
        head_sums = put_heads(3, left2, crossed_left2, head_sums)
        far_a, far_b, crossed_right2, head_sums = together(
            far_a, far_b, crossed_right2, head_sums
        )
        gate_sum, up_sum, down_sum = mlp_sums
        gate_sum, up_sum = gate_sum.T, up_sum.T
        small_rows = [v[-16:-12] for v in pieces]
        far_a, far_b, small_rows = together(far_a, far_b, small_rows)
        from_all = in_order(small_rows)
        count = tokens * local_heads
        d_rate_all = from_all[:, :count].reshape(segs * tokens, local_heads)
        small = [dot(normed_all, d_rate_all, 0, 0), jnp.sum(d_rate_all.astype(F32), axis=0)]
        for v in (scale_part, post_gain_part, post_bias_part):
            n = v.shape[0]
            both = from_all[:, count : count + 2 * n].astype(F32).reshape(2 * segs, n)
            small.append(jnp.sum(both, axis=0))
            count += 2 * n
        far2 = jnp.concatenate([far_a, far_b], axis=0)
        crossed_far2 = shift(far2, 0, 1)
        head_sums = put_heads(1, right2, crossed_right2, head_sums)
        query_sum, key_sum, value_sum, pre_sum, out_sum = put_heads(
            2, far2, crossed_far2, head_sums
        )
        pieces = (
            second, right2, far2, left2, crossed2, crossed_right2, crossed_far2, crossed_left2
        )
        norms = in_order([v[-16:-12] for v in pieces]).astype(F32)
        gain_grads = jnp.sum(norms.reshape(segs, 2, 2, model_width), axis=(0, 2))
    else:
        grads = (
            dot(hidden, group_cot),
            dot(mlp_group, d_gate_mlp, 0, 1),
            dot(mlp_group, d_up_mlp, 0, 1),
            dot(group_in, d_query, 0, 0),
            dot(group_in, d_key, 0, 0),
            dot(group_in, d_value, 0, 0),
            dot(group_in, d_gate_pre, 0, 0),
            out_weight_grad,
        )
        sums = lax.psum(tuple(g.astype(BF) for g in grads), "seq")
        down_sum, gate_sum, up_sum, query_sum, key_sum, value_sum, pre_sum, out_sum = (
            s.astype(F32) for s in sums
        )
        small = lax.psum(
            (
                dot(group_in, d_rate_pre, 0, 0),
                jnp.sum(d_rate_pre.astype(F32), axis=0),
                scale_part,
                post_gain_part,
                post_bias_part,
            ),
            "seq",
        )
        gain_grads = lax.psum((norm1_part, norm2_part), everywhere)
    return (
        block_out,
        input_grad,
        gain_grads[0],
        query_sum,
        key_sum,
        value_sum,
        pre_sum,
        small[0],
        small[1],
        small[2],
        init_grad[:, :HW, :HW],
        init_grad[:, HW, :HW],
        small[3],
        small[4],
        out_sum,
        gain_grads[1],
        gate_sum,
        up_sum,
        down_sum,
    )


def solution(mesh):
    in_specs = (
        P(("seq", "head"), None),
        P(),
        P(None, "head"),
        P(None, "head"),
        P(None, "head"),
        P(None, "head"),
        P(None, "head"),
        P("head"),
        P("head"),
        P("head", None, None),
        P("head", None),
        P("head"),
        P("head"),
        P("head", None),
        P(),
        P(None, "head"),
        P(None, "head"),
        P("head", None),
        P(("seq", "head"), None),
    )
    out_specs = (
        P(("seq", "head"), None),
        P(("seq", "head"), None),
        P(),
        P(None, "head"),
        P(None, "head"),
        P(None, "head"),
        P(None, "head"),
        P(None, "head"),
        P("head"),
        P("head"),
        P("head", None, None),
        P("head", None),
        P("head"),
        P("head"),
        P("head", None),
        P(),
        P(None, "head"),
        P(None, "head"),
        P("head", None),
    )
    return jax.shard_map(body, mesh=mesh, in_specs=in_specs, out_specs=out_specs, check_vma=False)
```

```python
import functools
import jax, jax.numpy as jnp
from jax import lax
from jax.experimental import pallas as pl
from jax.experimental.pallas import tpu as pltpu
from jax.sharding import PartitionSpec as P

CHUNK=128
MB=16
F32=jnp.float32; BF=jnp.bfloat16
LN=128
HW=64
VL=48*1024*1024

def mm(a,b,ca,cb):
    return lax.dot_general(a.astype(BF),b.astype(BF),(((ca,),(cb,)),((),())),preferred_element_type=F32)
def nn(a,b): return mm(a,b,1,0)
def nt(a,b): return mm(a,b,1,1)
def tn(a,b): return mm(a,b,0,0)
def split(a):
    hi=a.astype(BF)
    return hi,(a-hi.astype(F32)).astype(BF)
def nn3(a,b):
    ah,al=a; bh,bl=b
    return nn(ah,bh)+(nn(ah,bl)+nn(al,bh))

def lanes(shape): return lax.broadcasted_iota(jnp.int32,shape,1)
def rows(shape): return lax.broadcasted_iota(jnp.int32,shape,0)
def head_of(x,odd):
    y=pltpu.roll(x,HW,1) if odd else x
    return jnp.where(lanes(x.shape)<HW,y,0.0)
def aug(x): return jnp.where(lanes(x.shape)==HW,1.0,x)
def pair(a,b):
    return jnp.where(lanes(a.shape)<HW,a,pltpu.roll(b,HW,1))
def column(block,h):
    return jnp.sum(jnp.where(lanes(block.shape)==h,block,0.0),axis=1,keepdims=True)
def causal(C): return rows((C,C))>=lanes((C,C))
def earlier(C): return (rows((C,C))>>4)>(lanes((C,C))>>4)
def level(C,b):
    i=rows((C,C)); j=lanes((C,C))
    return ((i>>(b+1))==(j>>(b+1)))&((i>>b)>(j>>b))

def block_inverses(lows,C):
    b=4
    mask=level(C,b)
    ys=[jnp.where(mask,-low,0.0) for low in lows]
    b+=1
    while (1<<b)<C:
        mask=level(C,b)
        parts=[jnp.where(mask,low,0.0) for low in lows]
        yb=[y.astype(BF) for y in ys]
        zs=[p+nn(y,p) for y,p in zip(yb,parts)]
        ys=[y-(z+nn(z,b2)) for y,z,b2 in zip(ys,zs,yb)]
        b+=1
    return ys

def map_kernel(C,k_ref,v_ref,r_ref,t_ref,uw_ref,x_ref,y_ref):
    p=pl.program_id(0)
    N=k_ref.shape[0]
    last=y_ref.shape[0]-1
    @pl.when(p==0)
    def _(): y_ref[last]=jnp.zeros((80,LN),BF)
    units=[(odd,c,pl.ds(c*C,C)) for c in range(N//C) for odd in range(2)]
    mask=earlier(C)
    eye=jnp.where(rows((C,C))==lanes((C,C)),1.0,0.0)
    ks=[head_of(k_ref[sl,:],odd) for odd,c,sl in units]
    kws=[jnp.concatenate([aug(k),head_of(v_ref[sl,:],odd)-k],axis=1) for k,(odd,c,sl) in zip(ks,units)]
    krs=[(kw[:,:LN]*column(r_ref[sl,:],2*p+odd)).astype(BF) for kw,(odd,c,sl) in zip(kws,units)]
    lows=[jnp.where(mask,nt(kw[:,:LN],kr),0.0) for kw,kr in zip(kws,krs)]
    ys=block_inverses(lows,C)
    total=[None,None]
    uws=[kw+nn(y,kw) for y,kw in zip(ys,kws)]
    xcs=[tn(kr,jnp.where(lanes(uw.shape)<LN,-uw,uw)) for kr,uw in zip(krs,uws)]
    for (odd,c,sl),y,uw,xc in zip(units,ys,uws,xcs):
        t_ref[odd,c]=(y+eye).astype(BF)
        uw_ref[odd,sl,:]=uw.astype(BF)
        x_ref[odd,c]=xc.astype(BF)
        total[odd]=xc if total[odd] is None else total[odd]+xc+nn(xc[:,:LN],total[odd])
    for odd in range(2):
        h=2*p+odd
        a=total[odd][:,:LN]; o=total[odd][:,LN:]
        y_ref[h]=pair(a,o)[:80].astype(BF)
        col=jnp.sum(jnp.where(lanes(a.shape)==HW,a,0.0),axis=1,keepdims=True)[:80]
        y_ref[last]=jnp.where(lanes((80,LN))==h,col,y_ref[last].astype(F32)).astype(BF)

def local_kernel(C,q_ref,k_ref,r_ref,t_ref,uw_ref,qe_ref,zo_ref,pt_ref,vv_ref):
    p=pl.program_id(0)
    N=q_ref.shape[0]
    mask=causal(C)
    for c in range(N//C):
        sl=pl.ds(c*C,C)
        offs=[]
        for odd in range(2):
            h=2*p+odd
            q=head_of(q_ref[sl,:],odd); qa=aug(q)
            ka=aug(head_of(k_ref[sl,:],odd))
            kr=ka*column(r_ref[sl,:],h)
            pm=jnp.where(mask,nt(qa,kr),0.0)
            t=t_ref[odd,c]
            puw=nn(pm,uw_ref[odd,sl,:])
            qe_ref[odd,sl,:]=(qa-puw[:,:LN]).astype(BF)
            offs.append(q+puw[:,LN:])
            pt_ref[odd,c]=nn(pm,t).astype(BF)
            vv_ref[odd,sl,:]=tn(t,kr).astype(BF)
        zo_ref[sl,:]=pair(offs[0],offs[1])

def unpack(y,yb,h):
    y=y.astype(F32)
    col=column(yb.astype(F32),h)
    ln=lanes(y.shape)
    a=jnp.where(ln<HW,y,jnp.where(ln==HW,col,0.0))
    o=jnp.where(ln<HW,pltpu.roll(y,HW,1),0.0)
    pad=jnp.zeros((LN-80,LN),F32)
    return jnp.concatenate([a,pad],0),jnp.concatenate([o,pad],0)

def start_of(is_ref,ib_ref,odd):
    s=jnp.concatenate([is_ref[odd],ib_ref[odd],jnp.zeros((LN-HW-1,HW),F32)],axis=0)
    return jnp.concatenate([s,jnp.zeros_like(s)],axis=1)

def forward_kernel(C,seg_ref,y_ref,yb_ref,is_ref,ib_ref,x_ref,uw_ref,qe_ref,zo_ref,z_ref,e_ref,s_ref):
    p=pl.program_id(0)
    N=zo_ref.shape[0]
    segs=y_ref.shape[0]
    seg=seg_ref[0]
    nc=N//C
    ss=[start_of(is_ref,ib_ref,odd) for odd in range(2)]
    for j in range(segs-1):
        at=seg_ref[1+j]
        on=jnp.where(j<seg,1.0,0.0)
        for odd in range(2):
            a,o=unpack(y_ref[at,odd],yb_ref[at,0],2*p+odd)
            ss[odd]=ss[odd]+on*(nn(a,ss[odd])+o)
    sbs=[[],[]]
    for c in range(nc):
        for odd in range(2):
            sb=ss[odd].astype(BF)
            sbs[odd].append(sb)
            x=x_ref[odd,c]
            ss[odd]=ss[odd]+nn(x[:,:LN],sb)+x[:,LN:].astype(F32)
    for c in range(nc):
        sl=pl.ds(c*C,C)
        add=[]
        for odd in range(2):
            sb=sbs[odd][c]
            s_ref[odd,c]=sb
            uw=uw_ref[odd,sl,:]
            e_ref[odd,sl,:]=(nn(uw[:,:LN],sb)-uw[:,LN:].astype(F32)).astype(BF)
            add.append(nn(qe_ref[odd,sl,:],sb))
        z_ref[sl,:]=zo_ref[sl,:]+pair(add[0],add[1])

def state_grad_kernel(C,dz_ref,qe_ref,x_ref,d_ref,dseg_ref):
    N=dz_ref.shape[0]
    outs=[]
    for odd in range(2):
        g=jnp.zeros((LN,LN),F32)
        for c in reversed(range(N//C)):
            sl=pl.ds(c*C,C)
            dz=head_of(dz_ref[sl,:],odd)
            d=tn(qe_ref[odd,sl,:],dz)
            d_ref[odd,c]=d
            g=g+tn(x_ref[odd,c][:,:LN],g)+d
        outs.append(g)
    dseg_ref[0]=pair(outs[0],outs[1])[:80].astype(BF)

def query_grad_kernel(C,q_ref,k_ref,r_ref,dz_ref,e_ref,s_ref,pt_ref,dq_ref,b_ref,l_ref):
    p=pl.program_id(0)
    N=q_ref.shape[0]
    mask=causal(C)
    for c in range(N//C):
        sl=pl.ds(c*C,C)
        outs=[]
        for odd in range(2):
            h=2*p+odd
            dz=head_of(dz_ref[sl,:],odd); dzb=dz.astype(BF)
            qa=aug(head_of(q_ref[sl,:],odd))
            ka=aug(head_of(k_ref[sl,:],odd))
            kr=ka*column(r_ref[sl,:],h)
            fu=jnp.where(mask,-nt(dzb,e_ref[odd,sl,:]),0.0).astype(BF)
            outs.append(dz+nt(dzb,s_ref[odd,c])+nn(fu,kr))
            b_ref[odd,sl,:]=tn(fu,qa).astype(BF)
            l_ref[odd,sl,:]=-tn(pt_ref[odd,c],dzb)
        dq_ref[sl,:]=pair(outs[0],outs[1]).astype(BF)

def key_grad_kernel(C,seg_ref,y_ref,yb_ref,da_ref,k_ref,r_ref,e_ref,s_ref,vv_ref,b_ref,l_ref,x_ref,d_ref,dq_ref,dg_ref,dk_ref,dv_ref,dr_ref,gi_ref,pk_ref):
    p=pl.program_id(0)
    N=k_ref.shape[0]
    segs=y_ref.shape[0]
    seg=seg_ref[0]
    @pl.when(p==0)
    def _(): dr_ref[...]=jnp.zeros_like(dr_ref)
    pad=jnp.zeros((LN-80,LN),F32)
    nc=N//C
    full=[jnp.zeros((LN,LN),F32) for _ in range(2)]
    gs=[jnp.zeros((LN,LN),F32) for _ in range(2)]
    for j in reversed(range(segs)):
        at=seg_ref[1+j]
        for odd in range(2):
            a,_=unpack(y_ref[at,odd],yb_ref[at,0],2*p+odd)
            d=jnp.concatenate([head_of(da_ref[at,0].astype(F32),odd),pad],0)
            full[odd]=full[odd]+tn(a,full[odd])+d
            gs[odd]=jnp.where(j==seg+1,full[odd],gs[odd])
    for odd in range(2): gi_ref[odd]=full[odd][:72]
    gbs=[[None]*nc for _ in range(2)]
    for c in reversed(range(nc)):
        for odd in range(2):
            gb=gs[odd].astype(BF)
            gbs[odd][c]=gb
            gs[odd]=gs[odd]+tn(x_ref[odd,c][:,:LN],gb)+d_ref[odd,c]
    mask=earlier(C)
    for c in range(nc):
        sl=pl.ds(c*C,C)
        dks=[]; lams=[]
        for odd in range(2):
            h=2*p+odd
            gb=gbs[odd][c]
            ka=aug(head_of(k_ref[sl,:],odd))
            r=column(r_ref[sl,:],h)
            kr=ka*r
            e=e_ref[odd,sl,:]
            lam=l_ref[odd,sl,:]-nn(vv_ref[odd,sl,:],gb)
            lb=lam.astype(BF)
            hu=jnp.where(mask,-nt(lb,e),0.0).astype(BF)
            b=b_ref[odd,sl,:].astype(F32)+tn(hu,ka)-nt(e,gb)
            dks.append(r*b+nt(lb,s_ref[odd,c])+nn(hu,kr)+lam)
            lams.append(lam)
            dr=jnp.sum(ka*b,axis=1,keepdims=True)
            dr_ref[sl,:]=jnp.where(lanes((C,dr_ref.shape[1]))==h,dr,dr_ref[sl,:])
        dk_ref[sl,:]=pair(dks[0],dks[1]).astype(BF)
        dv_ref[sl,:]=-pair(lams[0],lams[1]).astype(BF)
        dq=dq_ref[sl,:].astype(F32); dg=dg_ref[sl,:].astype(F32)
        for odd in range(2):
            first=pair(head_of(dq,odd),dks[odd]); second=pair(-lams[odd],head_of(dg,odd))
            pk_ref[odd,sl,:]=jnp.concatenate([first,second],axis=1).astype(BF)

def params(): return pltpu.CompilerParams(dimension_semantics=("arbitrary",),vmem_limit_bytes=VL)
def S(shape,dt): return jax.ShapeDtypeStruct(shape,dt)

def specs(N,hl,C):
    nc=N//C
    d={}
    d["row"]=pl.BlockSpec((N,LN),lambda p,*_:(0,p))
    d["rate"]=pl.BlockSpec((N,hl),lambda p,*_:(0,0))
    d["cc"]=pl.BlockSpec((2,nc,C,C),lambda p,*_:(p,0,0,0))
    d["n256"]=pl.BlockSpec((2,N,2*LN),lambda p,*_:(p,0,0))
    d["n128"]=pl.BlockSpec((2,N,LN),lambda p,*_:(p,0,0))
    d["x"]=pl.BlockSpec((2,nc,LN,2*LN),lambda p,*_:(p,0,0,0))
    d["s"]=pl.BlockSpec((2,nc,LN,LN),lambda p,*_:(p,0,0,0))
    d["y"]=pl.BlockSpec((hl+1,80,LN),lambda p,*_:(0,0,0))
    return d

def build(N,hl,segs,C=128):
    nc=N//C; sp=specs(N,hl,C); G=(hl//2,)
    w=hl*HW
    K={}
    K["map"]=pl.pallas_call(functools.partial(map_kernel,C),grid=G,in_specs=[sp["row"],sp["row"],sp["rate"]],
        out_specs=[sp["cc"],sp["n256"],sp["x"],sp["y"]],
        out_shape=[S((hl,nc,C,C),BF),S((hl,N,2*LN),BF),S((hl,nc,LN,2*LN),BF),S((hl+1,80,LN),BF)],compiler_params=params(),name="segment_maps")
    K["local"]=pl.pallas_call(functools.partial(local_kernel,C),grid=G,in_specs=[sp["row"],sp["row"],sp["rate"],sp["cc"],sp["n256"]],
        out_specs=[sp["n128"],sp["row"],sp["cc"],sp["n128"]],
        out_shape=[S((hl,N,LN),BF),S((N,w),F32),S((hl,nc,C,C),BF),S((hl,N,LN),BF)],compiler_params=params(),name="local_parts")
    yall=pl.BlockSpec((segs,2,80,LN),lambda p,*_:(0,p,0,0)); yball=pl.BlockSpec((segs,1,80,LN),lambda p,*_:(0,hl,0,0))
    dall=pl.BlockSpec((segs,1,80,LN),lambda p,*_:(0,p,0,0))
    ist=pl.BlockSpec((2,HW,HW),lambda p,*_:(p,0,0)); ibs=pl.BlockSpec((2,1,HW),lambda p,*_:(p,0,0))
    def gs(i,o): return pltpu.PrefetchScalarGridSpec(num_scalar_prefetch=1,grid=G,in_specs=i,out_specs=o)
    K["forward"]=pl.pallas_call(functools.partial(forward_kernel,C),grid_spec=gs([yall,yball,ist,ibs,sp["x"],sp["n256"],sp["n128"],sp["row"]],[sp["row"],sp["n128"],sp["s"]]),
        out_shape=[S((N,w),F32),S((hl,N,LN),BF),S((hl,nc,LN,LN),BF)],compiler_params=params(),name="forward_states")
    K["sgrad"]=pl.pallas_call(functools.partial(state_grad_kernel,C),grid=G,in_specs=[sp["row"],sp["n128"],sp["x"]],
        out_specs=[sp["s"],pl.BlockSpec((1,80,LN),lambda p:(p,0,0))],out_shape=[S((hl,nc,LN,LN),F32),S((hl//2,80,LN),BF)],compiler_params=params(),name="state_grads")
    K["qgrad"]=pl.pallas_call(functools.partial(query_grad_kernel,C),grid=G,in_specs=[sp["row"],sp["row"],sp["rate"],sp["row"],sp["n128"],sp["s"],sp["cc"]],
        out_specs=[sp["row"],sp["n128"],sp["n128"]],out_shape=[S((N,w),BF),S((hl,N,LN),BF),S((hl,N,LN),F32)],compiler_params=params(),name="query_grads")
    K["kgrad"]=pl.pallas_call(functools.partial(key_grad_kernel,C),grid_spec=gs([yall,yball,dall,sp["row"],sp["rate"],sp["n128"],sp["s"],sp["n128"],sp["n128"],sp["n128"],sp["x"],sp["s"],sp["row"],sp["row"]],
        [sp["row"],sp["row"],sp["rate"],pl.BlockSpec((2,72,LN),lambda p,*_:(p,0,0)),sp["n256"]]),
        out_shape=[S((N,w),BF),S((N,w),BF),S((N,hl),F32),S((hl,72,LN),F32),S((hl,N,2*LN),BF)],compiler_params=params(),name="key_grads")
    return K


EPSILON = 1e-06


def grid_of():
    seq = lax.axis_size("seq")
    x = max(lax.axis_size("head") // 2, 1)
    if seq % x:
        x = 1
    return seq // x, x


def shift(v, dz, dx):
    Z, X = grid_of()
    pairs = [(z * X + x, ((z + dz) % Z) * X + (x + dx) % X) for z in range(Z) for x in range(X)]
    return lax.ppermute(v, "seq", pairs)


def seq_gather(v, between, *later):
    Z, X = grid_of()
    i = lax.axis_index("seq")
    j = jnp.arange(Z * X, dtype=jnp.int32)
    if (Z, X) != (4, 2):
        return (lax.all_gather(v, "seq", axis=0, tiled=False), j), between
    other = shift(v, 0, 1)
    if later:
        other, later = together(other, later)
    both = jnp.stack([v, other])
    left = shift(both, 1, 0)
    right = shift(both, 3, 0)
    left, right, between = together(left, right, between)
    far0 = shift(left[:1], 1, 0)
    far1 = shift(right[1:], 3, 0)
    z, x = i // X, i % X
    every = jnp.concatenate([both, right, far0, far1, left])
    order = ((j // X - z) % Z) * X + (j % X - x) % X
    return (every, order, *later), between


def head_shift(v, dy, dc):
    H = lax.axis_size("head")
    Y = H // 2
    pairs = [(y * 2 + c, ((y + dy) % Y) * 2 + (c + dc) % 2) for y in range(Y) for c in range(2)]
    return lax.ppermute(v, "head", pairs)


def head_gather(v, across=None):
    H = lax.axis_size("head")
    if H != 4:
        return lax.all_gather(v, "head", axis=0, tiled=True)
    i = lax.axis_index("head")
    y, c = i // 2, i % 2
    mine = jnp.stack([v, head_shift(v, 1, 0) if across is None else across])
    other = head_shift(mine, 0, 1)
    a = jnp.where(c == 0, mine, other)
    b = jnp.where(c == 0, other, mine)
    rows = [jnp.where(y == 0, a[0], a[1]), jnp.where(y == 0, b[0], b[1])]
    rows += [jnp.where(y == 0, a[1], a[0]), jnp.where(y == 0, b[1], b[0])]
    return jnp.concatenate(rows, axis=0)


def head_scatter(v, hold=None):
    H = lax.axis_size("head")
    v = v.astype(BF)
    if H != 4:
        return lax.psum_scatter(v, "head", scatter_dimension=0, tiled=True).astype(F32)
    i = lax.axis_index("head")
    y, c = i // 2, i % 2
    v = v.reshape(2, 2, v.shape[0] // 4, v.shape[1])
    got = head_shift(jnp.where(c == 0, v[:, 1], v[:, 0]), 0, 1)
    half = (jnp.where(c == 0, v[:, 0], v[:, 1]).astype(F32) + got.astype(F32)).astype(BF)
    back = head_shift(jnp.where(y == 0, half[1], half[0]), 1, 0)
    if hold is not None:
        back, hold = together(back, hold)
    total = jnp.where(y == 0, half[0], half[1]).astype(F32) + back.astype(F32)
    return total if hold is None else (total, hold)


def gelu_tanh(values):
    return jax.nn.gelu(values, approximate=True)


def dot(a, b, ca=1, cb=0):
    return lax.dot_general(a, b, (((ca,), (cb,)), ((), ())), preferred_element_type=F32)


def together(*values):
    return lax.optimization_barrier(values)


def at(v, i, axis=0):
    return lax.dynamic_index_in_dim(v, i, axis, keepdims=False)


def plus(a, b):
    return (a.astype(F32) + b.astype(F32)).astype(BF)


def slices_kernel(at_ref, g0, u0, h0, g1, u1, h1, x_ref, c_ref, send_ref, keep_ref):
    rows = g0.shape[0]
    for g, u, h, out in ((g0, u0, h0, send_ref), (g1, u1, h1, keep_ref)):
        for t, (left, right) in enumerate(((g, x_ref), (u, x_ref), (h, c_ref))):
            out[pl.ds(t * rows, rows), :] = dot(left[...], right[...]).astype(BF)


def mlp_slices(k, rows, d_gate, d_up, hidden, mlp_group, cot_group):
    i = lax.axis_index("seq")
    z, x = i // 2, i % 2
    to = ((z + k) % 4) * 2
    which = jnp.stack([to + 1 - x, to + x]).astype(jnp.int32)
    N, D = mlp_group.shape
    tile = min(D, 512)
    act = [pl.BlockSpec((rows, N), lambda j, o, n=n: (o[n], 0)) for n in (0, 1)]
    col = pl.BlockSpec((N, tile), lambda j, o: (0, j))
    out = pl.BlockSpec((3 * rows, tile), lambda j, o: (0, j))
    return pl.pallas_call(
        slices_kernel,
        grid_spec=pltpu.PrefetchScalarGridSpec(
            num_scalar_prefetch=1,
            grid=(D // tile,),
            in_specs=[act[0]] * 3 + [act[1]] * 3 + [col, col],
            out_specs=[out, out],
        ),
        out_shape=[jax.ShapeDtypeStruct((3 * rows, D), BF)] * 2,
        compiler_params=params(),
        name="mlp_slices",
    )(which, d_gate, d_up, hidden, d_gate, d_up, hidden, mlp_group, cot_group)


def slots():
    i = lax.axis_index("seq")
    z, x = i // 2, i % 2
    zs = (z + jnp.arange(4, dtype=jnp.int32)) % 4
    return jnp.concatenate([zs * 2 + x, zs * 2 + 1 - x]).astype(jnp.int32)


def finish_kernel(plan, at_ref, *refs):
    pieces, outs, scratch = refs[:8], refs[8:-1], refs[-1]
    for out, (first, rows, turned) in zip(outs, plan):
        for slot, ref in enumerate(pieces):
            start = pl.multiple_of(at_ref[slot] * rows, 16)
            scratch[pl.ds(start, rows), :] = ref[pl.ds(first, rows), :].astype(F32)
        if turned:
            out[...] = scratch[pl.ds(0, out.shape[1]), :].T
        else:
            out[...] = scratch[pl.ds(0, out.shape[0]), :]


def finish(pieces, plan, widths, name):
    R, D = pieces[0].shape
    out_specs, out_shape = [], []
    for w, (_, _, turned) in zip(widths, plan):
        if turned:
            out_specs.append(pl.BlockSpec((LN, w), lambda i, o: (i, 0)))
            out_shape.append(jax.ShapeDtypeStruct((D, w), F32))
        else:
            out_specs.append(pl.BlockSpec((w, LN), lambda i, o: (0, i)))
            out_shape.append(jax.ShapeDtypeStruct((w, D), F32))
    return pl.pallas_call(
        functools.partial(finish_kernel, plan),
        grid_spec=pltpu.PrefetchScalarGridSpec(
            num_scalar_prefetch=1,
            grid=(D // LN,),
            in_specs=[pl.BlockSpec((R, LN), lambda i, o: (0, i))] * 8,
            out_specs=out_specs,
            scratch_shapes=[pltpu.VMEM((8 * max(p[1] for p in plan), LN), F32)],
        ),
        out_shape=out_shape,
        compiler_params=params(),
        name=name,
    )(slots(), *pieces)


def put_heads_kernel(at_ref, own_ref, other_ref, *refs):
    outs = refs[-5:]
    for t, out in enumerate(outs):
        own = own_ref[pl.ds(t * HW, HW), :].astype(F32)
        other = other_ref[pl.ds(t * HW, HW), :].astype(F32)
        even = at_ref[1] == 0
        both = jnp.concatenate([jnp.where(even, own, other), jnp.where(even, other, own)], axis=0)
        out[...] = both.T if t < 4 else both


def put_heads(k, own, other, before):
    i = lax.axis_index("seq")
    place = jnp.stack([(i // 2 + k) % 4, i % 2]).astype(jnp.int32)
    R, D = own.shape
    width = 8 * HW
    tile = min(D, 512)
    piece = pl.BlockSpec((R, tile), lambda j, o: (0, j))
    turned = pl.BlockSpec((tile, LN), lambda j, o: (j, o[0]))
    straight = pl.BlockSpec((LN, tile), lambda j, o: (o[0], j))
    before = [] if before is None else list(before)
    return pl.pallas_call(
        put_heads_kernel,
        grid_spec=pltpu.PrefetchScalarGridSpec(
            num_scalar_prefetch=1,
            grid=(D // tile,),
            in_specs=[piece, piece] + [pl.BlockSpec(memory_space=pl.ANY)] * len(before),
            out_specs=[turned] * 4 + [straight],
        ),
        out_shape=[jax.ShapeDtypeStruct((D, width), F32)] * 4
        + [jax.ShapeDtypeStruct((width, D), F32)],
        input_output_aliases={3 + n: n for n in range(len(before))},
        compiler_params=params(),
        name="put_heads",
    )(place, own, other, *before)


def rows_of(values, D):
    values = jnp.concatenate(values)
    return jnp.concatenate([values, jnp.zeros((16 * D - values.shape[0],), BF)]).reshape(16, D)


def in_order(pieces):
    i = lax.axis_index("seq")
    z, x = i // 2, i % 2
    j = jnp.arange(8, dtype=jnp.int32)
    slot = (j // 2 - z) % 4 + 4 * ((j % 2 - x) % 2)
    return jnp.stack(pieces)[slot].reshape(8, -1)


def halves(v):
    hi = v.astype(BF)
    return jnp.stack([hi, (v - hi.astype(F32)).astype(BF)])


def body(
    block_input,
    norm1_gain,
    query_weight,
    key_weight,
    value_weight,
    gate_weight,
    rate_weight,
    rate_bias,
    rate_scale,
    init_state,
    init_bias,
    post_gain,
    post_bias,
    out_weight,
    norm2_gain,
    mlp_gate,
    mlp_up,
    mlp_down,
    out_cotangent,
):
    local_heads = init_state.shape[0]
    model_width = block_input.shape[1]
    width = mlp_gate.shape[1]
    segs = lax.axis_size("seq")
    heads = lax.axis_size("head")
    tokens = block_input.shape[0] * heads
    K = build(tokens, local_heads, segs, CHUNK)
    seg = lax.axis_index("seq").astype(jnp.int32).reshape(1)
    wide = local_heads == segs and tokens * segs * model_width <= 1 << 23 and grid_of() == (4, 2)
    everywhere = ("seq", "head")

    input_f32 = block_input.astype(F32)
    scale_in = lax.rsqrt(jnp.mean(input_f32 * input_f32, axis=-1, keepdims=True) + EPSILON)
    unit_in = input_f32 * scale_in
    normed = (unit_in * norm1_gain).astype(BF)
    group_in = head_gather(normed)
    key_rows = dot(group_in, key_weight)
    value_rows = dot(group_in, value_weight)
    rate_pre = dot(group_in, rate_weight) + rate_bias
    rate_sig = jax.nn.sigmoid(rate_pre)
    rate_rows = rate_sig * rate_scale
    inv, uw, step_maps, seg_map = K["map"](key_rows, value_rows, rate_rows)
    cot_late, seg_map = together(out_cotangent, seg_map)
    cot_across = head_shift(cot_late, 1, 0) if heads == 4 else cot_late
    query_rows = dot(group_in, query_weight)
    local = K["local"](query_rows, key_rows, rate_rows, inv, uw)
    (all_maps, order), (local, cot_across) = seq_gather(seg_map, (local, cot_across))
    group_cot = head_gather(out_cotangent, cot_across)
    q_eff, z_off, pt, vv = local
    place = jnp.concatenate([seg, order])
    if wide:
        normed_late, all_maps = together(normed, all_maps)
        normed_all = lax.all_gather(normed_late, everywhere, axis=0, tiled=True)
    gate_pre = dot(group_in, gate_weight)
    z_rows, errors, states = K["forward"](
        place, all_maps, all_maps, init_state, init_bias[:, None, :], step_maps, uw, q_eff, z_off
    )
    stat_sums = lax.psum((jnp.sum(z_rows, axis=-1), jnp.sum(z_rows * z_rows, axis=-1)), "head")
    row_mean = stat_sums[0] / model_width
    row_var = stat_sums[1] / model_width - row_mean * row_mean
    inv_scale = lax.rsqrt(row_var + EPSILON)[:, None]
    z_hat = (z_rows - row_mean[:, None]) * inv_scale
    post_out = z_hat * post_gain + post_bias
    gate_act, gelu_back = jax.vjp(gelu_tanh, gate_pre)
    gated_out = (gate_act * post_out).astype(BF)
    middle = input_f32 + head_scatter(dot(gated_out, out_weight))
    scale_mid = lax.rsqrt(jnp.mean(middle * middle, axis=-1, keepdims=True) + EPSILON)
    unit_mid = middle * scale_mid
    mlp_input = (unit_mid * norm2_gain).astype(BF)
    mlp_group = head_gather(mlp_input)
    gate_mlp = dot(mlp_gate, mlp_group, 0, 1)
    up_mlp = dot(mlp_up, mlp_group, 0, 1)
    silu_gate, silu_back = jax.vjp(jax.nn.silu, gate_mlp)
    hidden = (silu_gate * up_mlp).astype(BF)
    d_hidden = dot(mlp_down, group_cot, 1, 1)
    d_gate_mlp = silu_back(d_hidden * up_mlp)[0].astype(BF)
    d_up_mlp = (d_hidden * silu_gate).astype(BF)
    if wide:
        rows = -(-width // (16 * segs)) * 16
        slices = lambda k: mlp_slices(k, rows, d_gate_mlp, d_up_mlp, hidden, mlp_group, group_cot)
        d_gate_mlp, (sent, kept2) = together(d_gate_mlp, slices(2))
        got2 = shift(sent, 0, 1)
    d_mlp_part = dot(d_gate_mlp, mlp_gate, 0, 1) + dot(d_up_mlp, mlp_up, 0, 1)
    if wide:
        d_mlp_input, (got2, (sent1, kept1)) = head_scatter(d_mlp_part, (got2, slices(1)))
    else:
        d_mlp_input = head_scatter(d_mlp_part)
    scaled_mid = d_mlp_input * norm2_gain
    norm2_part = jnp.sum(d_mlp_input * unit_mid, axis=0)
    d_middle = out_cotangent.astype(F32) + scale_mid * (
        scaled_mid - unit_mid * jnp.mean(scaled_mid * unit_mid, axis=-1, keepdims=True)
    )
    d_attn = d_middle.astype(BF)
    if wide:
        got1 = shift(sent1, 0, 1)
        far = plus(kept2, got2)
        h = far.shape[0] // 32 * 16
        a_far, b_far = shift(far[:h], 1, 0), shift(far[h:], 3, 0)
        across = head_shift(d_attn, 1, 0)
        across, got1, a_far, b_far = together(across, got1, a_far, b_far)
        d_attn_group = head_gather(d_attn, across)
        ahead = plus(kept1, got1)
        up = jnp.concatenate([plus(ahead[:h], a_far), ahead[h:]], axis=0)
        up, (sent, kept3) = together(up, slices(3))
        from_left, got3 = shift(up, 1, 0), shift(sent, 0, 1)
    else:
        d_attn_group = head_gather(d_attn)
    out_weight_grad = dot(gated_out, d_attn_group, 0, 0).astype(BF)
    d_attn_group, out_weight_grad = together(d_attn_group, out_weight_grad)
    d_gated = dot(d_attn_group, out_weight, 1, 1)
    d_post = d_gated * gate_act
    d_gate_pre = gelu_back(d_gated * post_out)[0].astype(BF)
    post_gain_part = jnp.sum(d_post * z_hat, axis=0)
    post_bias_part = jnp.sum(d_post, axis=0)
    d_zhat = d_post * post_gain
    back_sums = lax.psum((jnp.sum(d_zhat, axis=-1), jnp.sum(d_zhat * z_hat, axis=-1)), "head")
    d_z = inv_scale * (
        d_zhat - back_sums[0][:, None] / model_width - z_hat * (back_sums[1][:, None] / model_width)
    )
    mlp_out = head_scatter(dot(hidden, mlp_down, 0, 0))
    d_z, mlp_out = together(d_z, mlp_out)
    step_grads, seg_grad = K["sgrad"](d_z, q_eff, step_maps)
    query_parts = K["qgrad"](query_rows, key_rows, rate_rows, d_z, errors, states, pt)
    if wide:
        (all_grads, _, (sent, kept0)), query_parts = seq_gather(seg_grad, query_parts, slices(0))
        got0 = shift(sent, 0, 1)
        all_grads, got3, from_left, normed_all = together(all_grads, got3, from_left, normed_all)
        behind = plus(kept3, got3)
        down = jnp.concatenate([behind[:h], plus(behind[h:], b_far)], axis=0)
        from_right = shift(down, 3, 0)
        out_slice = lax.psum_scatter(out_weight_grad, "seq", scatter_dimension=0, tiled=True)
    else:
        (all_grads, _), query_parts = seq_gather(seg_grad, query_parts)
    d_query, b_part, lam_part = query_parts
    d_key, d_value, d_rate, init_grad, packed = K["kgrad"](
        place, all_maps, all_maps, all_grads, key_rows, rate_rows, errors, states, vv,
        b_part, lam_part, step_maps, step_grads, d_query, d_gate_pre,
    )
    if wide:
        packed, out_slice = together(packed, out_slice)
        first = from_left.astype(F32) + from_right.astype(F32)
        first = (first + kept0.astype(F32) + got0.astype(F32)).astype(BF)
    d_rate_pre = (d_rate * rate_scale * rate_sig * (1.0 - rate_sig)).astype(BF)
    scale_part = jnp.sum(d_rate * rate_sig, axis=0)
    total = dot(d_query, query_weight, 1, 1)
    total = total + dot(d_key, key_weight, 1, 1)
    total = total + dot(d_value, value_weight, 1, 1)
    total = total + dot(d_gate_pre, gate_weight, 1, 1)
    d_normed = head_scatter(total + dot(d_rate_pre, rate_weight, 1, 1))
    scaled_in = d_normed * norm1_gain
    norm1_part = jnp.sum(d_normed * unit_in, axis=0)
    input_grad = d_middle + scale_in * (
        scaled_in - unit_in * jnp.mean(scaled_in * unit_in, axis=-1, keepdims=True)
    )
    block_out = (middle + mlp_out).astype(BF)

    if wide:
        extra = [d_rate_pre.reshape(-1)]
        for v in (scale_part, post_gain_part, post_bias_part):
            extra.append(halves(v).reshape(-1))
        first = jnp.concatenate([first, rows_of(extra, model_width)], axis=0)
        crossed = shift(first, 0, 1)
        packed = lax.all_to_all(packed, "seq", split_axis=0, concat_axis=0, tiled=True)
        packed, crossed, first = together(packed, crossed, first)
        left = shift(first, 1, 0)
        packed = packed.reshape(segs * tokens, packed.shape[2])
        own = dot(packed, normed_all, 0, 0).astype(BF)
        norm_parts = lax.psum((norm1_part, norm2_part), "head")
        norm_rows = rows_of([halves(v).reshape(-1) for v in norm_parts], model_width)
        second = jnp.concatenate([own, out_slice, norm_rows], axis=0)
        crossed2 = shift(second, 0, 1)
        left, crossed2, first, second = together(left, crossed2, first, second)
        right, crossed_left = shift(first, 3, 0), shift(left, 0, 1)
        left, right, crossed_left = together(left, right, crossed_left)
        h = first.shape[0] // 32 * 16
        far_a, far_b = shift(left[:h], 1, 0), shift(right[h:], 3, 0)
        crossed_right = shift(right, 0, 1)
        far_a, far_b, crossed_right, second = together(far_a, far_b, crossed_right, second)
        far = jnp.concatenate([far_a, far_b], axis=0)
        crossed_far, left2 = shift(far, 0, 1), shift(second, 1, 0)
        head_sums = put_heads(0, second, crossed2, None)
        crossed_far, left2, second, head_sums = together(crossed_far, left2, second, head_sums)
        right2, crossed_left2 = shift(second, 3, 0), shift(left2, 0, 1)
        pieces = (first, right, far, left, crossed, crossed_right, crossed_far, crossed_left)
        plan = tuple((t * rows, rows, False) for t in range(3))
        mlp_sums = finish(pieces, plan, (width,) * 3, "mlp_finish")
        left2, right2, crossed_left2, mlp_sums = together(left2, right2, crossed_left2, mlp_sums)
        h = second.shape[0] // 32 * 16
        far_a, far_b = shift(left2[:h], 1, 0), shift(right2[h:], 3, 0)
        crossed_right2 = shift(right2, 0, 1)
        head_sums = put_heads(3, left2, crossed_left2, head_sums)
        head_sums, small_rows = together(head_sums, [v[-16:-12] for v in pieces])
        far_a, far_b, crossed_right2, head_sums = together(
            far_a, far_b, crossed_right2, head_sums
        )
        gate_sum, up_sum, down_sum = mlp_sums
        gate_sum, up_sum = gate_sum.T, up_sum.T
        from_all = in_order(small_rows)
        count = tokens * local_heads
        d_rate_all = from_all[:, :count].reshape(segs * tokens, local_heads)
        small = [dot(normed_all, d_rate_all, 0, 0), jnp.sum(d_rate_all.astype(F32), axis=0)]
        for v in (scale_part, post_gain_part, post_bias_part):
            n = v.shape[0]
            both = from_all[:, count : count + 2 * n].astype(F32).reshape(2 * segs, n)
            small.append(jnp.sum(both, axis=0))
            count += 2 * n
        far2 = jnp.concatenate([far_a, far_b], axis=0)
        crossed_far2 = shift(far2, 0, 1)
        head_sums = put_heads(1, right2, crossed_right2, head_sums)
        query_sum, key_sum, value_sum, pre_sum, out_sum = put_heads(
            2, far2, crossed_far2, head_sums
        )
        pieces = (
            second, right2, far2, left2, crossed2, crossed_right2, crossed_far2, crossed_left2
        )
        norms = in_order([v[-16:-12] for v in pieces]).astype(F32)
        gain_grads = jnp.sum(norms.reshape(segs, 2, 2, model_width), axis=(0, 2))
    else:
        grads = (
            dot(hidden, group_cot),
            dot(mlp_group, d_gate_mlp, 0, 1),
            dot(mlp_group, d_up_mlp, 0, 1),
            dot(group_in, d_query, 0, 0),
            dot(group_in, d_key, 0, 0),
            dot(group_in, d_value, 0, 0),
            dot(group_in, d_gate_pre, 0, 0),
            out_weight_grad,
        )
        sums = lax.psum(tuple(g.astype(BF) for g in grads), "seq")
        down_sum, gate_sum, up_sum, query_sum, key_sum, value_sum, pre_sum, out_sum = (
            s.astype(F32) for s in sums
        )
        small = lax.psum(
            (
                dot(group_in, d_rate_pre, 0, 0),
                jnp.sum(d_rate_pre.astype(F32), axis=0),
                scale_part,
                post_gain_part,
                post_bias_part,
            ),
            "seq",
        )
        gain_grads = lax.psum((norm1_part, norm2_part), everywhere)
    return (
        block_out,
        input_grad,
        gain_grads[0],
        query_sum,
        key_sum,
        value_sum,
        pre_sum,
        small[0],
        small[1],
        small[2],
        init_grad[:, :HW, :HW],
        init_grad[:, HW, :HW],
        small[3],
        small[4],
        out_sum,
        gain_grads[1],
        gate_sum,
        up_sum,
        down_sum,
    )


def solution(mesh):
    in_specs = (
        P(("seq", "head"), None),
        P(),
        P(None, "head"),
        P(None, "head"),
        P(None, "head"),
        P(None, "head"),
        P(None, "head"),
        P("head"),
        P("head"),
        P("head", None, None),
        P("head", None),
        P("head"),
        P("head"),
        P("head", None),
        P(),
        P(None, "head"),
        P(None, "head"),
        P("head", None),
        P(("seq", "head"), None),
    )
    out_specs = (
        P(("seq", "head"), None),
        P(("seq", "head"), None),
        P(),
        P(None, "head"),
        P(None, "head"),
        P(None, "head"),
        P(None, "head"),
        P(None, "head"),
        P("head"),
        P("head"),
        P("head", None, None),
        P("head", None),
        P("head"),
        P("head"),
        P("head", None),
        P(),
        P(None, "head"),
        P(None, "head"),
        P("head", None),
    )
    return jax.shard_map(body, mesh=mesh, in_specs=in_specs, out_specs=out_specs, check_vma=False)
```
